128 devices in a mesh: gx: 16 (over y, x), gy: 8 (over z, core).
Axes of the slice: x: 4, y: 4, z: 4, core: 2. Of those that a mesh axis runs over, the one named last changes fastest.
Arguments:
- tiles: bfloat16 [3, 8, 768, 8704], P(None, None, 'gy', 'gx'), may hold values from 0.099609375 to 4
- offsets: int32 [8, 16, 2], P('gy', 'gx'), may hold values from 0 to 32, as said below
- psf: float32 [3, 3, 31], replicated, may hold values from 0.05 to 1
Outputs:
- restored: float32 [3, 8, 512, 8192], P(None, None, 'gy', 'gx')
- level_one: float32 [3, 4, 256, 4096], P(None, None, 'gy', 'gx')
- level_two: float32 [3, 2, 128, 2048], P(None, None, 'gy', 'gx')
The draws below stay inside these ranges and needn't reach their ends.
Inputs may be any that keep to these rules, and one draw needn't show every extreme that they name: offsets[j, i, 0] is 0 for j = 0 and 32 for j = 7; offsets[j, i, 1] is 0 for i = 0 and 32 for i = 15.
All inputs are finite; a program needn't handle non-finite values.
Results may differ from the reference program's by a relative error of at most 0.0015.
Values may be sent and summed in bfloat16 or wider, within the bound.
A program may use at most 128 MiB of HBM per device.

```python
import math
import jax
import jax.numpy as jnp
from jax import lax

CHANNELS = 3
SLAB = 8
CY = 64
CX = 512
MARGIN = 32
TAPS = 31
ITERS = 2
HALF = 15
TY = 96
TX = 544
GRID_Y = 8
GRID_X = 16
NY = 512
NX = 8192


def draw_offsets(key, part):
    shape = (GRID_Y, GRID_X, 2)
    shifts = jax.random.randint(key, shape, 0, MARGIN + 1)
    rows = lax.broadcasted_iota(jnp.int32, shape, 0)
    cols = lax.broadcasted_iota(jnp.int32, shape, 1)
    which = lax.broadcasted_iota(jnp.int32, shape, 2)
    shifts = jnp.where((which == 0) & (rows == GRID_Y - 1), MARGIN, shifts)
    shifts = jnp.where((which == 1) & (cols == GRID_X - 1), MARGIN, shifts)
    shifts = jnp.where((which == 0) & (rows == 0), 0, shifts)
    shifts = jnp.where((which == 1) & (cols == 0), 0, shifts)
    return shifts.astype(jnp.int32)


def levels(stream_key, dims, pieces, least, top_value):
    gain, own = 1.0, jax.random.fold_in(stream_key, 6)
    for position, blocks in pieces:
        steps = jnp.exp(jax.random.uniform(jax.random.fold_in(own, position), (blocks,), jnp.float32, least / len(pieces), top_value / len(pieces)))
        gain = gain * jnp.repeat(steps, dims[position] // blocks).reshape([-1 if axis == position else 1 for axis in range(len(dims))])
    return gain


def setup_inputs(seed: int = 0) -> dict:
    key_of = jax.random.split(jax.random.key(seed), 4)
    return {
        "tiles": jnp.clip(jnp.exp(math.log(4.0) - 3.6927934 * jax.random.uniform(key_of[0], (CHANNELS, SLAB, GRID_Y * TY, GRID_X * TX), jnp.float32) ** levels(key_of[0], (CHANNELS, SLAB, GRID_Y * TY, GRID_X * TX), ((2, 8), (3, 16)), -0.2, 0.2)), 0.099609375, 4.0).astype(jnp.bfloat16),
        "offsets": draw_offsets(jax.random.fold_in(key_of[3], 71), 0),
        "psf": jnp.clip(jnp.exp(jax.random.uniform(key_of[2], (CHANNELS, 3, TAPS), jnp.float32, math.log(0.05), math.log(1.0))), 0.05, 1.0),
    }


HIGH = lax.Precision.HIGHEST
GAUSS = (0.0625, 0.25, 0.375, 0.25, 0.0625)


def correlate(field, taps, axis, stride, pad_lo, pad_hi):
    moved = jnp.moveaxis(field, axis, -1)
    lead = moved.shape[:-1]
    flat = moved.reshape((-1, 1, moved.shape[-1]))
    result = lax.conv_general_dilated(flat, taps.reshape((1, 1, -1)), (stride,), [(pad_lo, pad_hi)], dimension_numbers=("NCH", "OIH", "NCH"), precision=HIGH)
    return jnp.moveaxis(result.reshape(lead + (result.shape[-1],)), -1, axis)


def blur(field, taps):
    field = correlate(field, taps[0], 0, 1, HALF, HALF)
    field = correlate(field, taps[1], 1, 1, HALF, HALF)
    return correlate(field, taps[2], 2, 1, HALF, HALF)


def shrink(field):
    gauss = jnp.array(GAUSS, jnp.float32)
    for axis in range(3):
        field = correlate(field, gauss, axis, 2, 2, 2)
    return field


def reference(tiles, offsets, psf):
    canvas = jnp.zeros((CHANNELS, SLAB, NY + 2 * MARGIN, NX + 2 * MARGIN), jnp.float32)
    cover = jnp.zeros((NY + 2 * MARGIN, NX + 2 * MARGIN), jnp.float32)

    def place(index, carry):
        canvas, cover = carry
        index = jnp.asarray(index).astype(jnp.int32)
        row = index // GRID_X
        col = index % GRID_X
        top = (row * CY + offsets[row, col, 0]).astype(jnp.int32)
        left = (col * CX + offsets[row, col, 1]).astype(jnp.int32)
        zero = jnp.zeros((), jnp.int32)
        block = lax.dynamic_slice(tiles, (zero, zero, (row * TY).astype(jnp.int32), (col * TX).astype(jnp.int32)), (CHANNELS, SLAB, TY, TX)).astype(jnp.float32)
        before = lax.dynamic_slice(canvas, (zero, zero, top, left), (CHANNELS, SLAB, TY, TX))
        canvas = lax.dynamic_update_slice(canvas, before + block, (zero, zero, top, left))
        seen = lax.dynamic_slice(cover, (top, left), (TY, TX))
        cover = lax.dynamic_update_slice(cover, seen + 1.0, (top, left))
        return canvas, cover

    canvas, cover = lax.fori_loop(0, GRID_Y * GRID_X, place, (canvas, cover))
    joined = canvas[:, :, :NY, :NX] / cover[:NY, :NX]
    kern = psf / jnp.sum(psf, axis=-1, keepdims=True)

    def channel(pair):
        field, taps = pair
        estimate = field
        for step in range(ITERS):
            ratio = field / blur(estimate, taps)
            estimate = estimate * blur(ratio, taps[:, ::-1])
        fine = shrink(estimate)
        coarse = shrink(fine)
        return estimate, fine, coarse

    restored, level_one, level_two = lax.map(channel, (joined, kern))
    return restored, level_one, level_two
```

```python
import jax
import jax.numpy as jnp
import numpy as np
from jax import lax
from jax.experimental import pallas as pl
from jax.experimental.pallas import tpu as pltpu
from jax.sharding import PartitionSpec as P

MESH = pl.DeviceIdType.MESH
F32 = jnp.float32
BF16 = jnp.bfloat16

CH, NZ, ROWS, COLS = 3, 8, 64, 512
MARGIN = 32
TROWS, TCOLS = ROWS + MARGIN, COLS + MARGIN
TAPS, HALF = 31, 15
ITERS = 2
STEPS = 2 * ITERS + 1
EDGE = 16
LANES = 128
OWN, STRIP = NZ * ROWS, NZ * EDGE
ALL = OWN + 2 * STRIP

GAUSS = np.array([1.0, 4.0, 6.0, 4.0, 1.0]) / 16.0


def _shrink(size_out, inputs):
    tap = np.asarray(inputs)[None, :] - 2 * np.arange(size_out)[:, None] + 2
    return np.where((tap >= 0) & (tap < 5), GAUSS[np.clip(tap, 0, 4)], 0.0)


def _shrink_twice(size_out, inputs, low_edge, high_edge):
    mid = np.arange(-2, 2 * size_out + 1)
    first = np.asarray(inputs)[None, :] - 2 * mid[:, None] + 2
    first = np.where((first >= 0) & (first < 5), GAUSS[np.clip(first, 0, 4)], 0.0)
    second = mid[None, :] - 2 * np.arange(size_out)[:, None] + 2
    second = np.where((second >= 0) & (second < 5), GAUSS[np.clip(second, 0, 4)], 0.0)
    keep = np.ones(mid.size)
    if low_edge:
        keep[mid < 0] = 0.0
    if high_edge:
        keep[mid >= 2 * size_out] = 0.0
    return second @ (keep[:, None] * first)


def _pyramid_rows():
    z_in = np.arange(NZ)
    z_one = _shrink(NZ // 2, z_in)
    z_two = _shrink(NZ // 4, np.arange(NZ // 2)) @ z_one
    parts = []
    for low, high in ((False, False), (True, False), (False, True)):
        blocks = []
        for coords, live in (
            (np.arange(ROWS), True),
            (np.arange(-EDGE, 0), not low),
            (np.arange(ROWS, ROWS + EDGE), not high),
        ):
            one = _shrink(ROWS // 2, coords) * live
            two = _shrink_twice(ROWS // 4, coords, low, high) * live
            blocks.append(np.concatenate([np.kron(z_one, one), np.kron(z_two, two)], axis=0))
        parts.append(np.concatenate(blocks, axis=1))
    return np.stack(parts).astype(jnp.bfloat16)


def _pyramid_cols():
    lane = np.arange(LANES)
    far = 10 * COLS
    edge = np.where(lane >= LANES - EDGE, lane - LANES, np.where(lane < EDGE, COLS + lane, far))
    coords = np.concatenate([edge, np.arange(COLS)])
    one = _shrink(COLS // 2, coords).T
    twos = [
        _shrink_twice(COLS // 4, coords, low, high).T
        for low, high in ((False, False), (True, False), (False, True))
    ]
    return one.astype(jnp.bfloat16), np.stack(twos).astype(jnp.bfloat16)


def _iota(shape, dim):
    return lax.broadcasted_iota(jnp.int32, shape, dim)


def _kernel(
    sizes,
    offsets_ref,
    psf_ref,
    tiles_ref,
    prow_ref,
    pone_ref,
    ptwo_ref,
    est_ref,
    one_ref,
    two_ref,
    shifted,
    own,
    low_send,
    low_recv,
    side_send,
    side_recv,
    info_send,
    info_recv,
    recip,
    joined,
    cur,
    top_recv,
    bot_recv,
    pack_right,
    pack_left,
    left_recv,
    right_recv,
    edge,
    spread,
    mat_x,
    mat_zy,
    join_send_sem,
    join_recv_sem,
    info_send_sem,
    info_recv_sem,
    send_sem,
    recv_sem,
):
    n_gx, n_gy = sizes
    gx, gy = lax.axis_index("gx"), lax.axis_index("gy")
    east, west = lax.rem(gx + 1, n_gx), lax.rem(gx + n_gx - 1, n_gx)
    south, north = lax.rem(gy + 1, n_gy), lax.rem(gy + n_gy - 1, n_gy)

    def at(x, y):
        return {"gx": x, "gy": y}

    around = [
        at(east, gy),
        at(west, gy),
        at(gx, south),
        at(gx, north),
        at(east, south),
        at(east, north),
        at(west, south),
        at(west, north),
    ]
    barrier = pltpu.get_barrier_semaphore()
    for place in around:
        pl.semaphore_signal(barrier, inc=1, device_id=place, device_id_type=MESH)
    pl.semaphore_wait(barrier, len(around))

    def remote(src, dst, send, recv, place):
        return pltpu.make_async_remote_copy(
            src_ref=src, dst_ref=dst, send_sem=send, recv_sem=recv, device_id=place, device_id_type=MESH
        )

    def join_copies(c):
        return [
            remote(low_send.at[c], low_recv.at[c], join_send_sem.at[c, 0], join_recv_sem.at[c, 0], around[2]),
            remote(side_send.at[c, 0], side_recv.at[c, 0], join_send_sem.at[c, 1], join_recv_sem.at[c, 1], around[0]),
            remote(side_send.at[c, 1], side_recv.at[c, 1], join_send_sem.at[c, 2], join_recv_sem.at[c, 2], around[4]),
        ]

    def info_copies():
        return [
            remote(info_send, info_recv.at[n], info_send_sem.at[n], info_recv_sem.at[n], around[k])
            for n, k in enumerate((0, 2, 4))
        ]

    def halo_copies(s, c):
        first, last = pl.ds(0, EDGE), pl.ds(ROWS - EDGE, EDGE)
        main, upper, lower = pl.ds(0, ROWS), pl.ds(ROWS, EDGE), pl.ds(ROWS + EDGE, EDGE)
        right, left = pack_right.at[s, c], pack_left.at[s, c]
        parts = [
            (cur.at[s, c, :, last], top_recv.at[s, c], around[2]),
            (cur.at[s, c, :, first], bot_recv.at[s, c], around[3]),
            (right, left_recv.at[s, c, main], around[0]),
            (left, right_recv.at[s, c, main], around[1]),
            (pack_right.at[s, c, last], left_recv.at[s, c, upper], around[4]),
            (pack_right.at[s, c, first], left_recv.at[s, c, lower], around[5]),
            (pack_left.at[s, c, last], right_recv.at[s, c, upper], around[6]),
            (pack_left.at[s, c, first], right_recv.at[s, c, lower], around[7]),
        ]
        return [
            remote(src, dst, send_sem.at[s, c, n], recv_sem.at[s, c, n], place)
            for n, (src, dst, place) in enumerate(parts)
        ]

    top = offsets_ref[0, 0, 0]
    left = offsets_ref[0, 0, 1]
    info_send[0:8] = jnp.full((8, LANES), top.astype(F32), F32)
    info_send[8:16] = jnp.full((8, LANES), left.astype(F32), F32)
    for copy in info_copies():
        copy.start()

    def one_hot(cond):
        return jnp.where(cond, 1.0, 0.0).astype(BF16)

    half = COLS // 2
    shift_a = one_hot(_iota((half, half), 1) - _iota((half, half), 0) == left)
    shift_b = one_hot(_iota((384, half), 1) - _iota((384, half), 0) + LANES == left)
    shift_c = one_hot(_iota((160, LANES), 1) - _iota((160, LANES), 0) + LANES == left)
    row, col = _iota((4 * ROWS, 2 * TROWS), 0), _iota((4 * ROWS, 2 * TROWS), 1)
    row_odd = lax.rem(row, 2 * ROWS) >= ROWS
    col_odd = col >= TROWS
    row_at = lax.rem(row, ROWS) + jnp.where(row >= 2 * ROWS, ROWS, 0)
    col_at = col - jnp.where(col_odd, TROWS, 0)
    lower_it = one_hot((row_odd == col_odd) & (row_at - col_at == top))

    def dot(a, b):
        return jnp.dot(a, b, preferred_element_type=F32)

    @pl.loop(0, CH)
    def _(c):
        tile = tiles_ref[c].reshape(NZ * TROWS, TCOLS)
        shifted[:, 0:half] = dot(tile[:, 0:half], shift_a).astype(BF16)
        shifted[:, half:COLS] = dot(tile[:, LANES:COLS], shift_b).astype(BF16)
        shifted[:, COLS:] = dot(tile[:, COLS - LANES :], shift_c).astype(BF16)
        for p in range(NZ // 2):
            placed = dot(lower_it, shifted[2 * p * TROWS : 2 * (p + 1) * TROWS, :])
            for zz in range(2):
                own[c, 2 * p + zz] = placed[zz * ROWS : (zz + 1) * ROWS, :COLS].astype(BF16)
                low_send[c, 2 * p + zz] = placed[(2 + zz) * ROWS : (3 + zz) * ROWS, :COLS].astype(BF16)
            for part in range(2):
                even = placed[2 * part * ROWS : (2 * part + 1) * ROWS, COLS:]
                odd = placed[(2 * part + 1) * ROWS : (2 * part + 2) * ROWS, COLS:]
                side_send[c, part, p] = (even + pltpu.roll(odd, 64, 1)).astype(BF16)
        for copy in join_copies(c):
            copy.start()

    @pl.loop(0, CH)
    def _(c):
        def total(a):
            t = psf_ref[c, a, 0]
            for k in range(1, TAPS):
                t = t + psf_ref[c, a, k]
            return t

        inv_x = 1.0 / jnp.full((1, LANES), total(2), F32)
        inv_zy = 1.0 / jnp.full((1, LANES), total(0) * total(1), F32)

        def banded(axis, diff, ks=range(TAPS)):
            ahead = jnp.zeros(diff.shape, F32)
            back = jnp.zeros(diff.shape, F32)
            for k in ks:
                hit = diff == k
                ahead = jnp.where(hit, psf_ref[c, axis, k], ahead)
                back = jnp.where(hit, psf_ref[c, axis, TAPS - 1 - k], back)
            return ahead, back

        square = (LANES, LANES)
        across = _iota(square, 0) - _iota(square, 1)
        for a, shift in enumerate((-113, 15, 143)):
            for d, block in enumerate(banded(2, across + shift)):
                block = (block * inv_x).astype(BF16)
                mat_x[d, c, a * LANES : (a + 1) * LANES, 0:LANES] = block
                mat_x[d, c, (a + 1) * LANES : (a + 2) * LANES, LANES:] = block
        zero = jnp.zeros(square, BF16)
        for d in range(2):
            mat_x[d, c, 0:LANES, LANES:] = zero
            mat_x[d, c, 3 * LANES :, 0:LANES] = zero

        yo = _iota((ROWS, LANES), 0)
        lane = _iota((ROWS, LANES), 1)
        inner = banded(1, lax.rem(lane, ROWS) - yo + HALF)
        above = banded(1, lax.rem(lane, EDGE) - EDGE - yo + HALF)
        below = banded(1, lax.rem(lane, EDGE) + ROWS - yo + HALF)
        has_above = jnp.where(gy > 0, 1.0, 0.0).astype(F32)
        has_below = jnp.where(gy < n_gy - 1, 1.0, 0.0).astype(F32)
        zo = _iota((NZ, LANES), 0)
        zlane = _iota((NZ, LANES), 1)
        depth_taps = range(HALF - NZ + 1, HALF + NZ)
        depth_own = [
            banded(0, 2 * j + lax.div(zlane, ROWS) - zo + HALF, depth_taps) for j in range(4)
        ]
        depth_edge = banded(0, lax.div(zlane, EDGE) - zo + HALF, depth_taps)
        for d in range(2):
            y_own = inner[d] * inv_zy
            y_above = above[d] * inv_zy * has_above
            y_below = below[d] * inv_zy * has_below
            for z in range(NZ):
                at_rows = slice(z * ROWS, (z + 1) * ROWS)
                for j in range(4):
                    mat_zy[d, c, at_rows, j * LANES : (j + 1) * LANES] = (
                        y_own * depth_own[j][d][z : z + 1]
                    ).astype(BF16)
                mat_zy[d, c, at_rows, 4 * LANES : 5 * LANES] = (
                    y_above * depth_edge[d][z : z + 1]
                ).astype(BF16)
                mat_zy[d, c, at_rows, 5 * LANES :] = (y_below * depth_edge[d][z : z + 1]).astype(BF16)

    for copy in info_copies():
        copy.wait_recv()
    has_west = jnp.where(gx > 0, 1.0, 0.0).astype(F32)
    has_north = jnp.where(gy > 0, 1.0, 0.0).astype(F32)
    r = _iota((ROWS, COLS), 0).astype(F32)
    x = _iota((ROWS, COLS), 1).astype(F32)

    def told(n):
        t = jnp.broadcast_to(info_recv[n, 0:1, 0:1], (ROWS, COLS))
        l = jnp.broadcast_to(info_recv[n, 8:9, 0:1], (ROWS, COLS))
        return t, l

    def covers(cond):
        return jnp.where(cond, 1.0, 0.0)

    count = covers((r >= top.astype(F32)) & (x >= left.astype(F32)))
    t, l = told(0)
    count = count + has_west * covers((r >= t) & (x < l + float(MARGIN)))
    t, l = told(1)
    count = count + has_north * covers((r < t + float(MARGIN)) & (x >= l))
    t, l = told(2)
    count = count + has_west * has_north * covers((r < t + float(MARGIN)) & (x < l + float(MARGIN)))
    recip[...] = 1.0 / count

    lane = _iota((ROWS, LANES), 1)

    def pack_edges(s, c, plane):
        right = jnp.zeros((ROWS, LANES), F32)
        left_side = jnp.zeros((ROWS, LANES), F32)
        for z in range(NZ):
            here = lax.div(lane, EDGE) == z
            field = plane(z)
            right = jnp.where(
                here, pltpu.roll(field[:, COLS - LANES :], (EDGE * z + EDGE) % LANES, 1), right
            )
            left_side = jnp.where(here, pltpu.roll(field[:, :LANES], EDGE * z, 1), left_side)
        pack_right[s, c] = right.astype(BF16)
        pack_left[s, c] = left_side.astype(BF16)

    @pl.loop(0, CH)
    def _(c):
        for copy in join_copies(c):
            copy.wait_recv()
        for z in range(NZ):
            total = own[c, z].astype(F32) + has_north * low_recv[c, z].astype(F32)
            spill = has_west * (
                side_recv[c, 0, z // 2].astype(F32) + has_north * side_recv[c, 1, z // 2].astype(F32)
            )
            if z % 2:
                spill = pltpu.roll(spill, 64, 1)
            spill = jnp.where(lane < 64, spill, 0.0)
            total = jnp.concatenate([total[:, :LANES] + spill, total[:, LANES:]], axis=1)
            value = total * recip[...]
            joined[c, z] = value
            est_ref[c, z] = value
            cur[0, c, z] = value.astype(BF16)
        pack_edges(0, c, lambda z: joined[c, z])
        for copy in halo_copies(0, c):
            copy.start()

    wide_lane = _iota((ROWS + 2 * EDGE, LANES), 1)
    from_west = (wide_lane >= LANES - EDGE) & (gx > 0)
    from_east = (wide_lane < EDGE) & (gx < n_gx - 1)

    def unpack_edges(s, c):
        west_side = left_recv[s, c].astype(F32)
        east_side = right_recv[s, c].astype(F32)
        for z in range(NZ):
            tile = jnp.where(
                from_west,
                pltpu.roll(west_side, (2 * LANES - EDGE - EDGE * z) % LANES, 1),
                jnp.where(from_east, pltpu.roll(east_side, (LANES - EDGE * z) % LANES, 1), 0.0),
            ).astype(BF16)
            edge[z * ROWS : (z + 1) * ROWS] = tile[:ROWS]
            edge[OWN + z * EDGE : OWN + (z + 1) * EDGE] = tile[ROWS : ROWS + EDGE]
            edge[OWN + STRIP + z * EDGE : OWN + STRIP + (z + 1) * EDGE] = tile[ROWS + EDGE :]

    def segments(s, c):
        return (
            (0, OWN, cur[s, c].reshape(OWN, COLS)),
            (OWN, STRIP, top_recv[s, c].reshape(STRIP, COLS)),
            (OWN + STRIP, STRIP, bot_recv[s, c].reshape(STRIP, COLS)),
        )

    def blur(d, s, c):
        unpack_edges(s, c)
        taps = mat_x[d, c]
        for start, size, field in segments(s, c):
            side = edge[start : start + size]
            first = jnp.concatenate([side, field[:, : COLS - LANES]], axis=1)
            spread[start : start + size, :half] = dot(first, taps).astype(BF16)
            second = jnp.concatenate([field[:, LANES:], side], axis=1)
            spread[start : start + size, half:] = dot(second, taps).astype(BF16)

    @pl.loop(0, ITERS)
    def _(it):
        for d in range(2):
            s = 2 * it + d

            @pl.loop(0, CH)
            def _(c):
                for copy in halo_copies(s, c):
                    copy.wait_recv()
                blur(d, s, c)
                for z in range(0, NZ, 2):
                    seen = dot(mat_zy[d, c, z * ROWS : (z + 2) * ROWS], spread[...])
                    seen = seen.reshape(2, ROWS, COLS)
                    if d == 0:
                        value = joined[c, z : z + 2] / seen
                    else:
                        value = est_ref[c, z : z + 2] * seen
                        est_ref[c, z : z + 2] = value
                    cur[s + 1, c, z : z + 2] = value.astype(BF16)
                pack_edges(s + 1, c, lambda z: cur[s + 1, c, z].astype(F32))
                for copy in halo_copies(s + 1, c):
                    copy.start()

    rows_of = jnp.where(gy == 0, prow_ref[1], jnp.where(gy == n_gy - 1, prow_ref[2], prow_ref[0]))
    cols_of = jnp.where(gx == 0, ptwo_ref[1], jnp.where(gx == n_gx - 1, ptwo_ref[2], ptwo_ref[0]))
    n_one = NZ * ROWS // 4
    last = STEPS - 1

    @pl.loop(0, CH)
    def _(c):
        for copy in halo_copies(last, c):
            copy.wait_recv()
        unpack_edges(last, c)
        main = jnp.zeros((rows_of.shape[0], COLS), F32)
        for start, size, field in segments(last, c):
            main = main + dot(rows_of[:, start : start + size], field)
        side = dot(rows_of, edge[...])
        tall = jnp.concatenate([side, main], axis=1).astype(BF16)
        one = dot(tall[:n_one], pone_ref[...])
        one_ref[c] = one.reshape(NZ // 2, ROWS // 2, COLS // 2)
        two = dot(tall[n_one:], cols_of)
        two_ref[c] = two.reshape(NZ // 4, ROWS // 4, COLS // 4)

    for copy in info_copies():
        copy.wait_send()

    @pl.loop(0, CH)
    def _(c):
        for copy in join_copies(c):
            copy.wait_send()

        @pl.loop(0, STEPS)
        def _(s):
            for copy in halo_copies(s, c):
                copy.wait_send()


def solution(mesh):
    import functools

    sizes = (mesh.shape["gx"], mesh.shape["gy"])
    prow = _pyramid_rows()
    pone, ptwo = _pyramid_cols()
    smem = pl.BlockSpec(memory_space=pltpu.SMEM)
    vmem = pl.BlockSpec(memory_space=pltpu.VMEM)
    dma = pltpu.SemaphoreType.DMA

    def per_device(tiles, offsets, psf):
        return pl.pallas_call(
            functools.partial(_kernel, sizes),
            out_shape=(
                jax.ShapeDtypeStruct((CH, NZ, ROWS, COLS), F32),
                jax.ShapeDtypeStruct((CH, NZ // 2, ROWS // 2, COLS // 2), F32),
                jax.ShapeDtypeStruct((CH, NZ // 4, ROWS // 4, COLS // 4), F32),
            ),
            in_specs=[smem, smem, vmem, vmem, vmem, vmem],
            out_specs=(vmem, vmem, vmem),
            scratch_shapes=[
                pltpu.VMEM((NZ * TROWS, COLS + LANES), BF16),
                pltpu.VMEM((CH, NZ, ROWS, COLS), BF16),
                pltpu.VMEM((CH, NZ, ROWS, COLS), BF16),
                pltpu.VMEM((CH, NZ, ROWS, COLS), BF16),
                pltpu.VMEM((CH, 2, NZ // 2, ROWS, LANES), BF16),
                pltpu.VMEM((CH, 2, NZ // 2, ROWS, LANES), BF16),
                pltpu.VMEM((16, LANES), F32),
                pltpu.VMEM((3, 16, LANES), F32),
                pltpu.VMEM((ROWS, COLS), F32),
                pltpu.VMEM((CH, NZ, ROWS, COLS), F32),
                pltpu.VMEM((STEPS, CH, NZ, ROWS, COLS), BF16),
                pltpu.VMEM((STEPS, CH, NZ, EDGE, COLS), BF16),
                pltpu.VMEM((STEPS, CH, NZ, EDGE, COLS), BF16),
                pltpu.VMEM((STEPS, CH, ROWS, LANES), BF16),
                pltpu.VMEM((STEPS, CH, ROWS, LANES), BF16),
                pltpu.VMEM((STEPS, CH, ROWS + 2 * EDGE, LANES), BF16),
                pltpu.VMEM((STEPS, CH, ROWS + 2 * EDGE, LANES), BF16),
                pltpu.VMEM((ALL, LANES), BF16),
                pltpu.VMEM((ALL, COLS), BF16),
                pltpu.VMEM((2, CH, COLS, COLS // 2), BF16),
                pltpu.VMEM((2, CH, OWN, ALL), BF16),
                dma((CH, 3)),
                dma((CH, 3)),
                dma((3,)),
                dma((3,)),
                dma((STEPS, CH, 8)),
                dma((STEPS, CH, 8)),
            ],
            compiler_params=pltpu.CompilerParams(
                collective_id=0, has_side_effects=True, vmem_limit_bytes=60 * 1024 * 1024
            ),
        )(offsets, psf, tiles, jnp.asarray(prow), jnp.asarray(pone), jnp.asarray(ptwo))

    in_specs = (P(None, None, "gy", "gx"), P("gy", "gx", None), P())
    out_specs = (P(None, None, "gy", "gx"),) * 3
    return jax.shard_map(
        per_device, mesh=mesh, in_specs=in_specs, out_specs=out_specs, check_vma=False
    )
```

```python
import functools

import jax
import jax.numpy as jnp
import numpy as np
from jax import lax
from jax.experimental import pallas as pl
from jax.experimental.pallas import tpu as pltpu
from jax.sharding import PartitionSpec as P

MESH = pl.DeviceIdType.MESH
F32 = jnp.float32
BF16 = jnp.bfloat16

CH, NZ, ROWS, COLS = 3, 8, 64, 512
MARGIN = 32
TROWS, TCOLS = ROWS + MARGIN, COLS + MARGIN
TAPS, HALF = 31, 15
ITERS = 2
STEPS = 2 * ITERS + 1
EDGE = 16
LANES = 128
OWN, STRIP = NZ * ROWS, NZ * EDGE
ALL = OWN + 2 * STRIP
GROUP = 4

GAUSS = np.array([1.0, 4.0, 6.0, 4.0, 1.0]) / 16.0


def _shrink(size_out, inputs):
    tap = np.asarray(inputs)[None, :] - 2 * np.arange(size_out)[:, None] + 2
    return np.where((tap >= 0) & (tap < 5), GAUSS[np.clip(tap, 0, 4)], 0.0)


def _shrink_twice(size_out, inputs, low_edge, high_edge):
    mid = np.arange(-2, 2 * size_out + 1)
    first = np.asarray(inputs)[None, :] - 2 * mid[:, None] + 2
    first = np.where((first >= 0) & (first < 5), GAUSS[np.clip(first, 0, 4)], 0.0)
    second = mid[None, :] - 2 * np.arange(size_out)[:, None] + 2
    second = np.where((second >= 0) & (second < 5), GAUSS[np.clip(second, 0, 4)], 0.0)
    keep = np.ones(mid.size)
    if low_edge:
        keep[mid < 0] = 0.0
    if high_edge:
        keep[mid >= 2 * size_out] = 0.0
    return second @ (keep[:, None] * first)


def _pyramid_rows():
    z_in = np.arange(NZ)
    z_one = _shrink(NZ // 2, z_in)
    z_two = _shrink(NZ // 4, np.arange(NZ // 2)) @ z_one
    parts = []
    for low, high in ((False, False), (True, False), (False, True)):
        blocks = []
        for coords, live in (
            (np.arange(ROWS), True),
            (np.arange(-EDGE, 0), not low),
            (np.arange(ROWS, ROWS + EDGE), not high),
        ):
            one = _shrink(ROWS // 2, coords) * live
            two = _shrink_twice(ROWS // 4, coords, low, high) * live
            blocks.append(np.concatenate([np.kron(z_one, one), np.kron(z_two, two)], axis=0))
        parts.append(np.concatenate(blocks, axis=1))
    return np.stack(parts).astype(jnp.bfloat16)


def _pyramid_cols():
    lane = np.arange(LANES)
    far = 10 * COLS
    edge = np.where(lane >= LANES - EDGE, lane - LANES, np.where(lane < EDGE, COLS + lane, far))
    coords = np.concatenate([edge, np.arange(COLS)])
    one = _shrink(COLS // 2, coords).T
    twos = [
        _shrink_twice(COLS // 4, coords, low, high).T
        for low, high in ((False, False), (True, False), (False, True))
    ]
    return one.astype(jnp.bfloat16), np.stack(twos).astype(jnp.bfloat16)


def _iota(shape, dim):
    return lax.broadcasted_iota(jnp.int32, shape, dim)


def _kernel(
    sizes,
    offsets_ref,
    psf_ref,
    tiles_ref,
    prow_ref,
    pone_ref,
    ptwo_ref,
    est_ref,
    one_ref,
    two_ref,
    tiles_in,
    prow_in,
    pone_in,
    ptwo_in,
    shifted,
    own,
    low_send,
    low_recv,
    side_send,
    side_recv,
    info_send,
    info_recv,
    recip,
    joined,
    cur,
    strip_recv,
    pack_right,
    pack_left,
    left_recv,
    right_recv,
    edge,
    spread,
    mat_x,
    mat_zy,
    load_sem,
    join_send_sem,
    join_recv_sem,
    info_send_sem,
    info_recv_sem,
    send_sem,
    recv_sem,
):
    n_gx, n_gy = sizes
    gx, gy = lax.axis_index("gx"), lax.axis_index("gy")
    east, west = lax.rem(gx + 1, n_gx), lax.rem(gx + n_gx - 1, n_gx)
    south, north = lax.rem(gy + 1, n_gy), lax.rem(gy + n_gy - 1, n_gy)

    def at(x, y):
        return {"gx": x, "gy": y}

    around = [
        at(east, gy),
        at(west, gy),
        at(gx, south),
        at(gx, north),
        at(east, south),
        at(east, north),
        at(west, south),
        at(west, north),
    ]
    barrier = pltpu.get_barrier_semaphore()
    for place in around:
        pl.semaphore_signal(barrier, inc=1, device_id=place, device_id_type=MESH)

    tile_loads = [
        pltpu.make_async_copy(tiles_ref.at[c], tiles_in.at[c], load_sem.at[c]) for c in range(CH)
    ]
    constant_loads = [
        pltpu.make_async_copy(src, dst, load_sem.at[CH + n])
        for n, (src, dst) in enumerate(
            ((prow_ref, prow_in), (pone_ref, pone_in), (ptwo_ref, ptwo_in))
        )
    ]
    for copy in tile_loads + constant_loads:
        copy.start()

    def remote(src, dst, send, recv, place):
        return pltpu.make_async_remote_copy(
            src_ref=src, dst_ref=dst, send_sem=send, recv_sem=recv, device_id=place, device_id_type=MESH
        )

    def join_copies(c):
        return [
            remote(low_send.at[c], low_recv.at[c], join_send_sem.at[c, 0], join_recv_sem.at[c, 0], around[2]),
            remote(side_send.at[c, 0], side_recv.at[c, 0], join_send_sem.at[c, 1], join_recv_sem.at[c, 1], around[0]),
            remote(side_send.at[c, 1], side_recv.at[c, 1], join_send_sem.at[c, 2], join_recv_sem.at[c, 2], around[4]),
        ]

    def info_copies():
        return [
            remote(info_send, info_recv.at[n], info_send_sem.at[n], info_recv_sem.at[n], around[k])
            for n, k in enumerate((0, 2, 4))
        ]

    def row_copies(s, c, planes=slice(0, NZ), rows=EDGE):
        z = pl.ds(planes.start, planes.stop - planes.start)
        parts = [
            (pl.ds(ROWS - rows, rows), 0, pl.ds(EDGE - rows, rows), around[2]),
            (pl.ds(0, rows), 1, pl.ds(0, rows), around[3]),
        ]
        return [
            remote(
                cur.at[s, c, z, src],
                strip_recv.at[s, c, n, z, dst],
                send_sem.at[s, c, n],
                recv_sem.at[s, c, n],
                place,
            )
            for src, n, dst, place in parts
        ]

    def edge_copies(s, c, rows=EDGE):
        first, last, main = pl.ds(0, rows), pl.ds(ROWS - rows, rows), pl.ds(0, ROWS)
        upper, lower = pl.ds(ROWS + EDGE - rows, rows), pl.ds(ROWS + EDGE, rows)
        right, left = pack_right.at[s, c], pack_left.at[s, c]
        parts = [
            (right, left_recv.at[s, c, main], around[0]),
            (left, right_recv.at[s, c, main], around[1]),
            (pack_right.at[s, c, last], left_recv.at[s, c, upper], around[4]),
            (pack_right.at[s, c, first], left_recv.at[s, c, lower], around[5]),
            (pack_left.at[s, c, last], right_recv.at[s, c, upper], around[6]),
            (pack_left.at[s, c, first], right_recv.at[s, c, lower], around[7]),
        ]
        return [
            remote(src, dst, send_sem.at[s, c, 2 + n], recv_sem.at[s, c, 2 + n], place)
            for n, (src, dst, place) in enumerate(parts)
        ]

    def start(copies):
        for copy in copies:
            copy.start()

    top = offsets_ref[0, 0, 0]
    left = offsets_ref[0, 0, 1]
    info_send[0:8] = jnp.full((8, LANES), top.astype(F32), F32)
    info_send[8:16] = jnp.full((8, LANES), left.astype(F32), F32)

    def one_hot(cond):
        return jnp.where(cond, 1.0, 0.0).astype(BF16)

    half = COLS // 2
    shift_a = one_hot(_iota((half, half), 1) - _iota((half, half), 0) == left)
    shift_b = one_hot(_iota((384, half), 1) - _iota((384, half), 0) + LANES == left)
    shift_c = one_hot(_iota((160, LANES), 1) - _iota((160, LANES), 0) + LANES == left)
    row, col = _iota((4 * ROWS, 2 * TROWS), 0), _iota((4 * ROWS, 2 * TROWS), 1)
    row_odd = lax.rem(row, 2 * ROWS) >= ROWS
    col_odd = col >= TROWS
    row_at = lax.rem(row, ROWS) + jnp.where(row >= 2 * ROWS, ROWS, 0)
    col_at = col - jnp.where(col_odd, TROWS, 0)
    lower_it = one_hot((row_odd == col_odd) & (row_at - col_at == top))

    def dot(a, b):
        return jnp.dot(a, b, preferred_element_type=F32)

    unused = jnp.zeros((CH, NZ, EDGE // 2, COLS), BF16)
    strip_recv[STEPS - 1, :, 0, :, : EDGE // 2] = unused
    strip_recv[STEPS - 1, :, 1, :, EDGE // 2 :] = unused
    unused = jnp.zeros((CH, EDGE // 2, LANES), BF16)
    for side_recv_ref in (left_recv, right_recv):
        side_recv_ref[STEPS - 1, :, ROWS : ROWS + EDGE // 2] = unused
        side_recv_ref[STEPS - 1, :, ROWS + EDGE + EDGE // 2 :] = unused

    pl.semaphore_wait(barrier, len(around))
    start(info_copies())

    @pl.loop(0, CH)
    def _(c):
        pltpu.make_async_copy(tiles_ref.at[c], tiles_in.at[c], load_sem.at[c]).wait()
        tile = tiles_in[c].reshape(NZ * TROWS, TCOLS)
        shifted[:, 0:half] = dot(tile[:, 0:half], shift_a).astype(BF16)
        shifted[:, half:COLS] = dot(tile[:, LANES:COLS], shift_b).astype(BF16)
        shifted[:, COLS:] = dot(tile[:, COLS - LANES :], shift_c).astype(BF16)
        for p in range(NZ // 2):
            placed = dot(lower_it, shifted[2 * p * TROWS : 2 * (p + 1) * TROWS, :])
            for zz in range(2):
                own[c, 2 * p + zz] = placed[zz * ROWS : (zz + 1) * ROWS, :COLS].astype(BF16)
                low_send[c, 2 * p + zz] = placed[(2 + zz) * ROWS : (3 + zz) * ROWS, :COLS].astype(BF16)
            for part in range(2):
                even = placed[2 * part * ROWS : (2 * part + 1) * ROWS, COLS:]
                odd = placed[(2 * part + 1) * ROWS : (2 * part + 2) * ROWS, COLS:]
                side_send[c, part, p] = (even + pltpu.roll(odd, 64, 1)).astype(BF16)
        start(join_copies(c))

    @pl.loop(0, CH)
    def _(c):
        def total(a):
            t = psf_ref[c, a, 0]
            for k in range(1, TAPS):
                t = t + psf_ref[c, a, k]
            return t

        inv_x = 1.0 / jnp.full((1, LANES), total(2), F32)
        inv_zy = 1.0 / jnp.full((1, LANES), total(0) * total(1), F32)

        def banded(axis, diff, ks=range(TAPS)):
            ahead = jnp.zeros(diff.shape, F32)
            back = jnp.zeros(diff.shape, F32)
            for k in ks:
                hit = diff == k
                ahead = jnp.where(hit, psf_ref[c, axis, k], ahead)
                back = jnp.where(hit, psf_ref[c, axis, TAPS - 1 - k], back)
            return ahead, back

        square = (LANES, LANES)
        across = _iota(square, 0) - _iota(square, 1)
        for a, shift in enumerate((-113, 15, 143)):
            for d, block in enumerate(banded(2, across + shift)):
                block = (block * inv_x).astype(BF16)
                mat_x[d, c, a * LANES : (a + 1) * LANES, 0:LANES] = block
                mat_x[d, c, (a + 1) * LANES : (a + 2) * LANES, LANES:] = block
        zero = jnp.zeros(square, BF16)
        for d in range(2):
            mat_x[d, c, 0:LANES, LANES:] = zero
            mat_x[d, c, 3 * LANES :, 0:LANES] = zero

        yo = _iota((ROWS, LANES), 0)
        lane = _iota((ROWS, LANES), 1)
        inner = banded(1, lax.rem(lane, ROWS) - yo + HALF)
        above = banded(1, lax.rem(lane, EDGE) - EDGE - yo + HALF)
        below = banded(1, lax.rem(lane, EDGE) + ROWS - yo + HALF)
        has_above = jnp.where(gy > 0, 1.0, 0.0).astype(F32)
        has_below = jnp.where(gy < n_gy - 1, 1.0, 0.0).astype(F32)
        zo = _iota((NZ, LANES), 0)
        zlane = _iota((NZ, LANES), 1)
        depth_taps = range(HALF - NZ + 1, HALF + NZ)
        depth_own = [
            banded(0, 2 * j + lax.div(zlane, ROWS) - zo + HALF, depth_taps) for j in range(4)
        ]
        depth_edge = banded(0, lax.div(zlane, EDGE) - zo + HALF, depth_taps)
        for d in range(2):
            y_own = inner[d] * inv_zy
            y_above = above[d] * inv_zy * has_above
            y_below = below[d] * inv_zy * has_below
            for z in range(NZ):
                at_rows = slice(z * ROWS, (z + 1) * ROWS)
                for j in range(4):
                    mat_zy[d, c, at_rows, j * LANES : (j + 1) * LANES] = (
                        y_own * depth_own[j][d][z : z + 1]
                    ).astype(BF16)
                mat_zy[d, c, at_rows, 4 * LANES : 5 * LANES] = (
                    y_above * depth_edge[d][z : z + 1]
                ).astype(BF16)
                mat_zy[d, c, at_rows, 5 * LANES :] = (y_below * depth_edge[d][z : z + 1]).astype(BF16)

    for copy in info_copies():
        copy.wait_recv()
    has_west = jnp.where(gx > 0, 1.0, 0.0).astype(F32)
    has_north = jnp.where(gy > 0, 1.0, 0.0).astype(F32)
    r = _iota((ROWS, COLS), 0).astype(F32)
    x = _iota((ROWS, COLS), 1).astype(F32)

    def told(n):
        t = jnp.broadcast_to(info_recv[n, 0:1, 0:1], (ROWS, COLS))
        l = jnp.broadcast_to(info_recv[n, 8:9, 0:1], (ROWS, COLS))
        return t, l

    def covers(cond):
        return jnp.where(cond, 1.0, 0.0)

    count = covers((r >= top.astype(F32)) & (x >= left.astype(F32)))
    t, l = told(0)
    count = count + has_west * covers((r >= t) & (x < l + float(MARGIN)))
    t, l = told(1)
    count = count + has_north * covers((r < t + float(MARGIN)) & (x >= l))
    t, l = told(2)
    count = count + has_west * has_north * covers((r < t + float(MARGIN)) & (x < l + float(MARGIN)))
    recip[...] = 1.0 / count

    lane = _iota((ROWS, LANES), 1)

    def pack_edges(s, c, plane):
        right = jnp.zeros((ROWS, LANES), F32)
        left_side = jnp.zeros((ROWS, LANES), F32)
        for z in range(NZ):
            here = lax.div(lane, EDGE) == z
            field = plane(z)
            right = jnp.where(
                here, pltpu.roll(field[:, COLS - LANES :], (EDGE * z + EDGE) % LANES, 1), right
            )
            left_side = jnp.where(here, pltpu.roll(field[:, :LANES], EDGE * z, 1), left_side)
        pack_right[s, c] = right.astype(BF16)
        pack_left[s, c] = left_side.astype(BF16)

    @pl.loop(0, CH)
    def _(c):
        for copy in join_copies(c):
            copy.wait_recv()
        for z in range(NZ):
            total = own[c, z].astype(F32) + has_north * low_recv[c, z].astype(F32)
            spill = has_west * (
                side_recv[c, 0, z // 2].astype(F32) + has_north * side_recv[c, 1, z // 2].astype(F32)
            )
            if z % 2:
                spill = pltpu.roll(spill, 64, 1)
            spill = jnp.where(lane < 64, spill, 0.0)
            total = jnp.concatenate([total[:, :LANES] + spill, total[:, LANES:]], axis=1)
            value = total * recip[...]
            joined[c, z] = value
            est_ref[c, z] = value
            cur[0, c, z] = value.astype(BF16)
        start(row_copies(0, c))
        pack_edges(0, c, lambda z: joined[c, z])
        start(edge_copies(0, c))

    wide_lane = _iota((ROWS + 2 * EDGE, LANES), 1)
    from_west = (wide_lane >= LANES - EDGE) & (gx > 0)
    from_east = (wide_lane < EDGE) & (gx < n_gx - 1)

    def unpack_edges(s, c):
        west_side = left_recv[s, c].astype(F32)
        east_side = right_recv[s, c].astype(F32)
        for z in range(NZ):
            tile = jnp.where(
                from_west,
                pltpu.roll(west_side, (2 * LANES - EDGE - EDGE * z) % LANES, 1),
                jnp.where(from_east, pltpu.roll(east_side, (LANES - EDGE * z) % LANES, 1), 0.0),
            ).astype(BF16)
            edge[z * ROWS : (z + 1) * ROWS] = tile[:ROWS]
            edge[OWN + z * EDGE : OWN + (z + 1) * EDGE] = tile[ROWS : ROWS + EDGE]
            edge[OWN + STRIP + z * EDGE : OWN + STRIP + (z + 1) * EDGE] = tile[ROWS + EDGE :]

    def segments(s, c):
        return (
            (0, OWN, cur[s, c].reshape(OWN, COLS)),
            (OWN, 2 * STRIP, strip_recv[s, c].reshape(2 * STRIP, COLS)),
        )

    def blur(d, s, c):
        unpack_edges(s, c)
        taps = mat_x[d, c]
        for begin, size, field in segments(s, c):
            side = edge[begin : begin + size]
            first = jnp.concatenate([side, field[:, : COLS - LANES]], axis=1)
            spread[begin : begin + size, :half] = dot(first, taps).astype(BF16)
            second = jnp.concatenate([field[:, LANES:], side], axis=1)
            spread[begin : begin + size, half:] = dot(second, taps).astype(BF16)

    last = STEPS - 1

    def iterate(it, d, final):
        s = 2 * it + d
        rows = EDGE // 2 if final else EDGE

        @pl.loop(0, CH)
        def _(c):
            for copy in row_copies(s, c) + edge_copies(s, c):
                copy.wait_recv()
            blur(d, s, c)
            for z in range(0, NZ, GROUP):
                planes = slice(z, z + GROUP)
                seen = dot(mat_zy[d, c, z * ROWS : (z + GROUP) * ROWS], spread[...])
                seen = seen.reshape(GROUP, ROWS, COLS)
                if d == 0:
                    value = joined[c, planes] / seen
                else:
                    value = est_ref[c, planes] * seen
                    est_ref[c, planes] = value
                cur[s + 1, c, planes] = value.astype(BF16)
                start(row_copies(s + 1, c, planes, rows))
            pack_edges(s + 1, c, lambda z: cur[s + 1, c, z].astype(F32))
            start(edge_copies(s + 1, c, rows))

    @pl.loop(0, ITERS - 1)
    def _(it):
        iterate(it, 0, False)
        iterate(it, 1, False)

    iterate(ITERS - 1, 0, False)
    iterate(ITERS - 1, 1, True)

    for copy in constant_loads:
        copy.wait()
    rows_of = jnp.where(gy == 0, prow_in[1], jnp.where(gy == n_gy - 1, prow_in[2], prow_in[0]))
    cols_of = jnp.where(gx == 0, ptwo_in[1], jnp.where(gx == n_gx - 1, ptwo_in[2], ptwo_in[0]))
    n_one = NZ * ROWS // 4

    @pl.loop(0, CH)
    def _(c):
        for copy in row_copies(last, c, rows=EDGE // 2) + edge_copies(last, c, EDGE // 2):
            copy.wait_recv()
        unpack_edges(last, c)
        main = jnp.zeros((rows_of.shape[0], COLS), F32)
        for begin, size, field in segments(last, c):
            main = main + dot(rows_of[:, begin : begin + size], field)
        side = dot(rows_of, edge[...])
        tall = jnp.concatenate([side, main], axis=1)
        high = tall.astype(BF16)
        low = (tall - high.astype(F32)).astype(BF16)
        one = dot(high[:n_one], pone_in[...]) + dot(low[:n_one], pone_in[...])
        one_ref[c] = one.reshape(NZ // 2, ROWS // 2, COLS // 2)
        two = dot(high[n_one:], cols_of) + dot(low[n_one:], cols_of)
        two_ref[c] = two.reshape(NZ // 4, ROWS // 4, COLS // 4)

    for copy in info_copies():
        copy.wait_send()

    @pl.loop(0, CH)
    def _(c):
        for copy in join_copies(c):
            copy.wait_send()

        @pl.loop(0, last)
        def _(s):
            for copy in row_copies(s, c) + edge_copies(s, c):
                copy.wait_send()

        for copy in row_copies(last, c, rows=EDGE // 2) + edge_copies(last, c, EDGE // 2):
            copy.wait_send()


def _settle(*refs):
    sem = refs[-1]
    copies = [pltpu.make_async_copy(refs[n], refs[n + 3], sem.at[n]) for n in range(3)]
    for copy in copies:
        copy.start()
    for copy in copies:
        copy.wait()


def solution(mesh):

    sizes = (mesh.shape["gx"], mesh.shape["gy"])
    prow = _pyramid_rows()
    pone, ptwo = _pyramid_cols()
    smem = pl.BlockSpec(memory_space=pltpu.SMEM)
    vmem = pl.BlockSpec(memory_space=pltpu.VMEM)
    hbm = pl.BlockSpec(memory_space=pltpu.HBM)
    dma = pltpu.SemaphoreType.DMA

    def per_device(tiles, offsets, psf):
        outs = pl.pallas_call(
            functools.partial(_kernel, sizes),
            out_shape=(
                pltpu.VMEM((CH, NZ, ROWS, COLS), F32),
                pltpu.VMEM((CH, NZ // 2, ROWS // 2, COLS // 2), F32),
                pltpu.VMEM((CH, NZ // 4, ROWS // 4, COLS // 4), F32),
            ),
            in_specs=[smem, smem, hbm, hbm, hbm, hbm],
            out_specs=(vmem, vmem, vmem),
            scratch_shapes=[
                pltpu.VMEM((CH, NZ, TROWS, TCOLS), BF16),
                pltpu.VMEM(prow.shape, BF16),
                pltpu.VMEM(pone.shape, BF16),
                pltpu.VMEM(ptwo.shape, BF16),
                pltpu.VMEM((NZ * TROWS, COLS + LANES), BF16),
                pltpu.VMEM((CH, NZ, ROWS, COLS), BF16),
                pltpu.VMEM((CH, NZ, ROWS, COLS), BF16),
                pltpu.VMEM((CH, NZ, ROWS, COLS), BF16),
                pltpu.VMEM((CH, 2, NZ // 2, ROWS, LANES), BF16),
                pltpu.VMEM((CH, 2, NZ // 2, ROWS, LANES), BF16),
                pltpu.VMEM((16, LANES), F32),
                pltpu.VMEM((3, 16, LANES), F32),
                pltpu.VMEM((ROWS, COLS), F32),
                pltpu.VMEM((CH, NZ, ROWS, COLS), F32),
                pltpu.VMEM((STEPS, CH, NZ, ROWS, COLS), BF16),
                pltpu.VMEM((STEPS, CH, 2, NZ, EDGE, COLS), BF16),
                pltpu.VMEM((STEPS, CH, ROWS, LANES), BF16),
                pltpu.VMEM((STEPS, CH, ROWS, LANES), BF16),
                pltpu.VMEM((STEPS, CH, ROWS + 2 * EDGE, LANES), BF16),
                pltpu.VMEM((STEPS, CH, ROWS + 2 * EDGE, LANES), BF16),
                pltpu.VMEM((ALL, LANES), BF16),
                pltpu.VMEM((ALL, COLS), BF16),
                pltpu.VMEM((2, CH, COLS, COLS // 2), BF16),
                pltpu.VMEM((2, CH, OWN, ALL), BF16),
                dma((CH + 3,)),
                dma((CH, 3)),
                dma((CH, 3)),
                dma((3,)),
                dma((3,)),
                dma((STEPS, CH, 8)),
                dma((STEPS, CH, 8)),
            ],
            compiler_params=pltpu.CompilerParams(
                collective_id=0, has_side_effects=True, vmem_limit_bytes=48 * 1024 * 1024
            ),
        )(*[
            pltpu.with_memory_space_constraint(x, pltpu.HBM)
            for x in (offsets, psf, tiles, jnp.asarray(prow), jnp.asarray(pone), jnp.asarray(ptwo))
        ])
        return pl.pallas_call(
            _settle,
            out_shape=tuple(jax.ShapeDtypeStruct(o.shape, o.dtype) for o in outs),
            in_specs=[vmem] * 3,
            out_specs=(hbm,) * 3,
            scratch_shapes=[dma((3,))],
            compiler_params=pltpu.CompilerParams(vmem_limit_bytes=4 * 1024 * 1024),
        )(*[pltpu.with_memory_space_constraint(o, pltpu.VMEM) for o in outs])

    in_specs = (P(None, None, "gy", "gx"), P("gy", "gx", None), P())
    out_specs = (P(None, None, "gy", "gx"),) * 3
    return jax.shard_map(
        per_device, mesh=mesh, in_specs=in_specs, out_specs=out_specs, check_vma=False
    )
```

```python
import functools

import jax
import jax.numpy as jnp
import numpy as np
from jax import lax
from jax.experimental import pallas as pl
from jax.experimental.pallas import tpu as pltpu
from jax.sharding import PartitionSpec as P

MESH = pl.DeviceIdType.MESH
F32 = jnp.float32
BF16 = jnp.bfloat16

CH, NZ, ROWS, COLS = 3, 8, 64, 512
MARGIN = 32
TROWS, TCOLS = ROWS + MARGIN, COLS + MARGIN
TAPS, HALF = 31, 15
ITERS = 2
STEPS = 2 * ITERS + 1
EDGE = 16
RELAY = 2
LANES = 128
OWN, STRIP = NZ * ROWS, NZ * EDGE
ALL = OWN + 2 * STRIP

GAUSS = np.array([1.0, 4.0, 6.0, 4.0, 1.0]) / 16.0


def _shrink(size_out, inputs):
    tap = np.asarray(inputs)[None, :] - 2 * np.arange(size_out)[:, None] + 2
    return np.where((tap >= 0) & (tap < 5), GAUSS[np.clip(tap, 0, 4)], 0.0)


def _shrink_twice(size_out, inputs, low_edge, high_edge):
    mid = np.arange(-2, 2 * size_out + 1)
    first = np.asarray(inputs)[None, :] - 2 * mid[:, None] + 2
    first = np.where((first >= 0) & (first < 5), GAUSS[np.clip(first, 0, 4)], 0.0)
    second = mid[None, :] - 2 * np.arange(size_out)[:, None] + 2
    second = np.where((second >= 0) & (second < 5), GAUSS[np.clip(second, 0, 4)], 0.0)
    keep = np.ones(mid.size)
    if low_edge:
        keep[mid < 0] = 0.0
    if high_edge:
        keep[mid >= 2 * size_out] = 0.0
    return second @ (keep[:, None] * first)


def _pyramid_rows():
    z_in = np.arange(NZ)
    z_one = _shrink(NZ // 2, z_in)
    z_two = _shrink(NZ // 4, np.arange(NZ // 2)) @ z_one
    parts = []
    for low, high in ((False, False), (True, False), (False, True)):
        blocks = []
        for coords, live in (
            (np.arange(ROWS), True),
            (np.arange(-EDGE, 0), not low),
            (np.arange(ROWS, ROWS + EDGE), not high),
        ):
            one = _shrink(ROWS // 2, coords) * live
            two = _shrink_twice(ROWS // 4, coords, low, high) * live
            blocks.append(np.concatenate([np.kron(z_one, one), np.kron(z_two, two)], axis=0))
        parts.append(np.concatenate(blocks, axis=1))
    return np.stack(parts).astype(jnp.bfloat16)


def _pyramid_cols():
    lane = np.arange(LANES)
    far = 10 * COLS
    edge = np.where(lane >= LANES - EDGE, lane - LANES, np.where(lane < EDGE, COLS + lane, far))
    coords = np.concatenate([edge, np.arange(COLS)])
    one = _shrink(COLS // 2, coords).T
    twos = [
        _shrink_twice(COLS // 4, coords, low, high).T
        for low, high in ((False, False), (True, False), (False, True))
    ]
    return one.astype(jnp.bfloat16), np.stack(twos).astype(jnp.bfloat16)


def _iota(shape, dim):
    return lax.broadcasted_iota(jnp.int32, shape, dim)


def _kernel(
    sizes,
    offsets_in,
    psf_in,
    tiles_ref,
    prow_ref,
    pone_ref,
    ptwo_ref,
    est_ref,
    one_ref,
    two_ref,
    offsets_ref,
    psf_ref,
    tiles_in,
    prow_in,
    pone_in,
    ptwo_in,
    shifted,
    own,
    low_send,
    low_recv,
    side_send,
    side_recv,
    info_send,
    info_recv,
    recip,
    joined,
    cur,
    strip_recv,
    pack_right,
    pack_left,
    left_recv,
    right_recv,
    edge,
    spread,
    mat_x,
    mat_zy,
    load_sem,
    join_send_sem,
    join_recv_sem,
    relay,
    relay_send_sem,
    relay_recv_sem,
    info_send_sem,
    info_recv_sem,
    send_sem,
    recv_sem,
):
    n_gx, n_gy = sizes
    gx, gy = lax.axis_index("gx"), lax.axis_index("gy")
    east, west = lax.rem(gx + 1, n_gx), lax.rem(gx + n_gx - 1, n_gx)
    south, north = lax.rem(gy + 1, n_gy), lax.rem(gy + n_gy - 1, n_gy)

    def at(x, y):
        return {"gx": x, "gy": y}

    around = [
        at(east, gy),
        at(west, gy),
        at(gx, south),
        at(gx, north),
        at(east, south),
        at(east, north),
        at(west, south),
        at(west, north),
    ]
    odd = lax.rem(gy, 2) == 1
    ring = [at(gx, lax.rem(gy + k, n_gy)) for k in (n_gy - 2, n_gy - 3, 2, 3)]
    barrier = pltpu.get_barrier_semaphore()
    for place in around + ring:
        pl.semaphore_signal(barrier, inc=1, device_id=place, device_id_type=MESH)

    tile_loads = [
        pltpu.make_async_copy(tiles_ref.at[c], tiles_in.at[c], load_sem.at[c]) for c in range(CH)
    ]
    constant_loads = [
        pltpu.make_async_copy(src, dst, load_sem.at[CH + n])
        for n, (src, dst) in enumerate(
            ((prow_ref, prow_in), (pone_ref, pone_in), (ptwo_ref, ptwo_in))
        )
    ]
    offsets_load = pltpu.make_async_copy(offsets_in, offsets_ref, load_sem.at[CH + 3])
    psf_load = pltpu.make_async_copy(psf_in, psf_ref, load_sem.at[CH + 4])
    for copy in [offsets_load, *tile_loads, psf_load, *constant_loads]:
        copy.start()

    def remote(src, dst, send, recv, place):
        return pltpu.make_async_remote_copy(
            src_ref=src, dst_ref=dst, send_sem=send, recv_sem=recv, device_id=place, device_id_type=MESH
        )

    def join_copies(c):
        return [
            remote(side_send.at[c, 0], side_recv.at[c, 0], join_send_sem.at[c, 1], join_recv_sem.at[c, 1], around[0]),
            remote(side_send.at[c, 1], side_recv.at[c, 1], join_send_sem.at[c, 2], join_recv_sem.at[c, 2], around[4]),
        ]

    def lower_copy(c, planes=slice(0, NZ - RELAY)):
        z = pl.ds(planes.start, planes.stop - planes.start)
        return remote(
            low_send.at[c, z], low_recv.at[c, z], join_send_sem.at[c, 0], join_recv_sem.at[c, 0], around[2]
        )

    far = pl.ds(NZ - RELAY, RELAY)

    def far_copy(c):
        return remote(
            low_send.at[c, far], low_recv.at[c, far], relay_send_sem.at[c, 0], relay_recv_sem.at[c, 0], around[2]
        )

    def relay_copy(c, hop):
        src = low_send.at[c, far] if hop == 0 else relay.at[c, hop - 1]
        dst = low_recv.at[c, far] if hop == 2 else relay.at[c, hop]
        return remote(
            src,
            dst,
            relay_send_sem.at[c, hop],
            relay_recv_sem.at[c, 0 if hop == 2 else hop + 1],
            ring[1] if hop == 2 else ring[0],
        )

    def info_copies():
        return [
            remote(info_send, info_recv.at[n], info_send_sem.at[n], info_recv_sem.at[n], around[k])
            for n, k in enumerate((0, 2, 4))
        ]

    def row_copies(s, c, rows=EDGE):
        parts = [
            (pl.ds(ROWS - rows, rows), 0, pl.ds(EDGE - rows, rows), around[2]),
            (pl.ds(0, rows), 1, pl.ds(0, rows), around[3]),
        ]
        return [
            remote(
                cur.at[s, c, :, src],
                strip_recv.at[s, c, n, :, dst],
                send_sem.at[s, c, n],
                recv_sem.at[s, c, n],
                place,
            )
            for src, n, dst, place in parts
        ]

    def edge_copies(s, c, rows=EDGE):
        first, last, main = pl.ds(0, rows), pl.ds(ROWS - rows, rows), pl.ds(0, ROWS)
        upper, lower = pl.ds(ROWS + EDGE - rows, rows), pl.ds(ROWS + EDGE, rows)
        right, left = pack_right.at[s, c], pack_left.at[s, c]
        parts = [
            (right, left_recv.at[s, c, main], around[0]),
            (left, right_recv.at[s, c, main], around[1]),
            (pack_right.at[s, c, last], left_recv.at[s, c, upper], around[4]),
            (pack_right.at[s, c, first], left_recv.at[s, c, lower], around[5]),
            (pack_left.at[s, c, last], right_recv.at[s, c, upper], around[6]),
            (pack_left.at[s, c, first], right_recv.at[s, c, lower], around[7]),
        ]
        return [
            remote(src, dst, send_sem.at[s, c, 2 + n], recv_sem.at[s, c, 2 + n], place)
            for n, (src, dst, place) in enumerate(parts)
        ]

    def start(copies):
        for copy in copies:
            copy.start()

    offsets_load.wait()
    top = offsets_ref[0, 0, 0]
    left = offsets_ref[0, 0, 1]
    info_send[0:8] = jnp.full((8, LANES), top.astype(F32), F32)
    info_send[8:16] = jnp.full((8, LANES), left.astype(F32), F32)

    def one_hot(cond):
        return jnp.where(cond, 1.0, 0.0).astype(BF16)

    half = COLS // 2
    shift_a = one_hot(_iota((half, half), 1) - _iota((half, half), 0) == left)
    shift_b = one_hot(_iota((384, half), 1) - _iota((384, half), 0) + LANES == left)
    shift_c = one_hot(_iota((160, LANES), 1) - _iota((160, LANES), 0) + LANES == left)
    row, col = _iota((4 * ROWS, 2 * TROWS), 0), _iota((4 * ROWS, 2 * TROWS), 1)
    row_odd = lax.rem(row, 2 * ROWS) >= ROWS
    col_odd = col >= TROWS
    row_at = lax.rem(row, ROWS) + jnp.where(row >= 2 * ROWS, ROWS, 0)
    col_at = col - jnp.where(col_odd, TROWS, 0)
    lower_it = one_hot((row_odd == col_odd) & (row_at - col_at == top))

    def dot(a, b):
        return jnp.dot(a, b, preferred_element_type=F32)

    unused = jnp.zeros((CH, NZ, EDGE // 2, COLS), BF16)
    strip_recv[STEPS - 1, :, 0, :, : EDGE // 2] = unused
    strip_recv[STEPS - 1, :, 1, :, EDGE // 2 :] = unused
    unused = jnp.zeros((CH, EDGE // 2, LANES), BF16)
    for side_recv_ref in (left_recv, right_recv):
        side_recv_ref[STEPS - 1, :, ROWS : ROWS + EDGE // 2] = unused
        side_recv_ref[STEPS - 1, :, ROWS + EDGE + EDGE // 2 :] = unused

    pl.semaphore_wait(barrier, len(around) + len(ring))
    start(info_copies())

    @pl.loop(0, CH)
    def _(c):
        pltpu.make_async_copy(tiles_ref.at[c], tiles_in.at[c], load_sem.at[c]).wait()
        tile = tiles_in[c].reshape(NZ * TROWS, TCOLS)
        shifted[:, 0:half] = dot(tile[:, 0:half], shift_a).astype(BF16)
        shifted[:, half:COLS] = dot(tile[:, LANES:COLS], shift_b).astype(BF16)
        shifted[:, COLS:] = dot(tile[:, COLS - LANES :], shift_c).astype(BF16)
        for p in (NZ // 2 - 1, *range(NZ // 2 - 1)):
            placed = dot(lower_it, shifted[2 * p * TROWS : 2 * (p + 1) * TROWS, :])
            for zz in range(2):
                own[c, 2 * p + zz] = placed[zz * ROWS : (zz + 1) * ROWS, :COLS].astype(BF16)
                low_send[c, 2 * p + zz] = placed[(2 + zz) * ROWS : (3 + zz) * ROWS, :COLS].astype(BF16)
            for part in range(2):
                even = placed[2 * part * ROWS : (2 * part + 1) * ROWS, COLS:]
                second = placed[(2 * part + 1) * ROWS : (2 * part + 2) * ROWS, COLS:]
                side_send[c, part, p] = (even + pltpu.roll(second, 64, 1)).astype(BF16)
            if 2 * p < NZ - RELAY:
                lower_copy(c, slice(2 * p, 2 * p + 2)).start()
            else:

                @pl.when(odd)
                def _():
                    relay_copy(c, 0).start()

                @pl.when(jnp.logical_not(odd))
                def _():
                    far_copy(c).start()

        start(join_copies(c))

    psf_load.wait()

    @pl.loop(0, CH)
    def _(c):
        def total(a):
            t = psf_ref[c, a, 0]
            for k in range(1, TAPS):
                t = t + psf_ref[c, a, k]
            return t

        inv_x = 1.0 / jnp.full((1, LANES), total(2), F32)
        inv_zy = 1.0 / jnp.full((1, LANES), total(0) * total(1), F32)

        def banded(axis, diff, ks=range(TAPS)):
            ahead = jnp.zeros(diff.shape, F32)
            back = jnp.zeros(diff.shape, F32)
            for k in ks:
                hit = diff == k
                ahead = jnp.where(hit, psf_ref[c, axis, k], ahead)
                back = jnp.where(hit, psf_ref[c, axis, TAPS - 1 - k], back)
            return ahead, back

        square = (LANES, LANES)
        across = _iota(square, 0) - _iota(square, 1)
        for a, shift in enumerate((-113, 15, 143)):
            for d, block in enumerate(banded(2, across + shift)):
                block = (block * inv_x).astype(BF16)
                mat_x[d, c, a * LANES : (a + 1) * LANES, 0:LANES] = block
                mat_x[d, c, (a + 1) * LANES : (a + 2) * LANES, LANES:] = block
        zero = jnp.zeros(square, BF16)
        for d in range(2):
            mat_x[d, c, 0:LANES, LANES:] = zero
            mat_x[d, c, 3 * LANES :, 0:LANES] = zero

        yo = _iota((ROWS, LANES), 0)
        lane = _iota((ROWS, LANES), 1)
        inner = banded(1, lax.rem(lane, ROWS) - yo + HALF)
        above = banded(1, lax.rem(lane, EDGE) - EDGE - yo + HALF)
        below = banded(1, lax.rem(lane, EDGE) + ROWS - yo + HALF)
        has_above = jnp.where(gy > 0, 1.0, 0.0).astype(F32)
        has_below = jnp.where(gy < n_gy - 1, 1.0, 0.0).astype(F32)
        zo = _iota((NZ, LANES), 0)
        zlane = _iota((NZ, LANES), 1)
        depth_taps = range(HALF - NZ + 1, HALF + NZ)
        depth_own = [
            banded(0, 2 * j + lax.div(zlane, ROWS) - zo + HALF, depth_taps) for j in range(4)
        ]
        depth_edge = banded(0, lax.div(zlane, EDGE) - zo + HALF, depth_taps)
        for d in range(2):
            y_own = inner[d] * inv_zy
            y_above = above[d] * inv_zy * has_above
            y_below = below[d] * inv_zy * has_below
            for z in range(NZ):
                at_rows = slice(z * ROWS, (z + 1) * ROWS)
                for j in range(4):
                    mat_zy[d, c, at_rows, j * LANES : (j + 1) * LANES] = (
                        y_own * depth_own[j][d][z : z + 1]
                    ).astype(BF16)
                mat_zy[d, c, at_rows, 4 * LANES : 5 * LANES] = (
                    y_above * depth_edge[d][z : z + 1]
                ).astype(BF16)
                mat_zy[d, c, at_rows, 5 * LANES :] = (y_below * depth_edge[d][z : z + 1]).astype(BF16)

        @pl.when(odd)
        def _():
            relay_copy(c, 0).wait_recv()
            relay_copy(c, 1).start()

    @pl.when(odd)
    def _():
        @pl.loop(0, CH)
        def _(c):
            relay_copy(c, 1).wait_recv()
            relay_copy(c, 2).start()

    for copy in info_copies():
        copy.wait_recv()
    has_west = jnp.where(gx > 0, 1.0, 0.0).astype(F32)
    has_north = jnp.where(gy > 0, 1.0, 0.0).astype(F32)
    r = _iota((ROWS, COLS), 0).astype(F32)
    x = _iota((ROWS, COLS), 1).astype(F32)

    def told(n):
        t = jnp.broadcast_to(info_recv[n, 0:1, 0:1], (ROWS, COLS))
        l = jnp.broadcast_to(info_recv[n, 8:9, 0:1], (ROWS, COLS))
        return t, l

    def covers(cond):
        return jnp.where(cond, 1.0, 0.0)

    count = covers((r >= top.astype(F32)) & (x >= left.astype(F32)))
    t, l = told(0)
    count = count + has_west * covers((r >= t) & (x < l + float(MARGIN)))
    t, l = told(1)
    count = count + has_north * covers((r < t + float(MARGIN)) & (x >= l))
    t, l = told(2)
    count = count + has_west * has_north * covers((r < t + float(MARGIN)) & (x < l + float(MARGIN)))
    recip[...] = 1.0 / count

    lane = _iota((ROWS, LANES), 1)

    def pack_edges(s, c, plane):
        right = jnp.zeros((ROWS, LANES), F32)
        left_side = jnp.zeros((ROWS, LANES), F32)
        for z in range(NZ):
            here = lax.div(lane, EDGE) == z
            field = plane(z)
            right = jnp.where(
                here, pltpu.roll(field[:, COLS - LANES :], (EDGE * z + EDGE) % LANES, 1), right
            )
            left_side = jnp.where(here, pltpu.roll(field[:, :LANES], EDGE * z, 1), left_side)
        pack_right[s, c] = right.astype(BF16)
        pack_left[s, c] = left_side.astype(BF16)

    @pl.loop(0, CH)
    def _(c):
        for copy in [lower_copy(c), far_copy(c), *join_copies(c)]:
            copy.wait_recv()
        for z in range(NZ):
            total = own[c, z].astype(F32) + has_north * low_recv[c, z].astype(F32)
            spill = has_west * (
                side_recv[c, 0, z // 2].astype(F32) + has_north * side_recv[c, 1, z // 2].astype(F32)
            )
            if z % 2:
                spill = pltpu.roll(spill, 64, 1)
            spill = jnp.where(lane < 64, spill, 0.0)
            total = jnp.concatenate([total[:, :LANES] + spill, total[:, LANES:]], axis=1)
            value = total * recip[...]
            joined[c, z] = value
            est_ref[c, z] = value
            cur[0, c, z] = value.astype(BF16)
        start(row_copies(0, c))
        pack_edges(0, c, lambda z: joined[c, z])
        start(edge_copies(0, c))

    wide_lane = _iota((ROWS + 2 * EDGE, LANES), 1)
    from_west = (wide_lane >= LANES - EDGE) & (gx > 0)
    from_east = (wide_lane < EDGE) & (gx < n_gx - 1)

    def unpack_edges(s, c):
        west_side = left_recv[s, c].astype(F32)
        east_side = right_recv[s, c].astype(F32)
        for z in range(NZ):
            tile = jnp.where(
                from_west,
                pltpu.roll(west_side, (2 * LANES - EDGE - EDGE * z) % LANES, 1),
                jnp.where(from_east, pltpu.roll(east_side, (LANES - EDGE * z) % LANES, 1), 0.0),
            ).astype(BF16)
            edge[z * ROWS : (z + 1) * ROWS] = tile[:ROWS]
            edge[OWN + z * EDGE : OWN + (z + 1) * EDGE] = tile[ROWS : ROWS + EDGE]
            edge[OWN + STRIP + z * EDGE : OWN + STRIP + (z + 1) * EDGE] = tile[ROWS + EDGE :]

    def segments(s, c):
        return (
            (0, OWN, cur[s, c].reshape(OWN, COLS)),
            (OWN, 2 * STRIP, strip_recv[s, c].reshape(2 * STRIP, COLS)),
        )

    def blur(d, s, c):
        unpack_edges(s, c)
        taps = mat_x[d, c]
        for begin, size, field in segments(s, c):
            side = edge[begin : begin + size]
            first = jnp.concatenate([side, field[:, : COLS - LANES]], axis=1)
            spread[begin : begin + size, :half] = dot(first, taps).astype(BF16)
            second = jnp.concatenate([field[:, LANES:], side], axis=1)
            spread[begin : begin + size, half:] = dot(second, taps).astype(BF16)

    last = STEPS - 1

    def iterate(it, d, final):
        s = 2 * it + d
        rows = EDGE // 2 if final else EDGE

        @pl.loop(0, CH)
        def _(c):
            for copy in row_copies(s, c) + edge_copies(s, c):
                copy.wait_recv()
            blur(d, s, c)
            seen = dot(mat_zy[d, c], spread[...]).reshape(NZ, ROWS, COLS)
            if d == 0:
                value = joined[c] / seen
            else:
                value = est_ref[c] * seen
                est_ref[c] = value
            cur[s + 1, c] = value.astype(BF16)
            pack_edges(s + 1, c, lambda z: cur[s + 1, c, z].astype(F32))
            start(edge_copies(s + 1, c, rows))
            start(row_copies(s + 1, c, rows))

    @pl.loop(0, ITERS - 1)
    def _(it):
        iterate(it, 0, False)
        iterate(it, 1, False)

    iterate(ITERS - 1, 0, False)
    iterate(ITERS - 1, 1, True)

    for copy in constant_loads:
        copy.wait()
    rows_of = jnp.where(gy == 0, prow_in[1], jnp.where(gy == n_gy - 1, prow_in[2], prow_in[0]))
    cols_of = jnp.where(gx == 0, ptwo_in[1], jnp.where(gx == n_gx - 1, ptwo_in[2], ptwo_in[0]))
    n_one = NZ * ROWS // 4

    @pl.loop(0, CH)
    def _(c):
        for copy in row_copies(last, c, EDGE // 2) + edge_copies(last, c, EDGE // 2):
            copy.wait_recv()
        unpack_edges(last, c)
        main = jnp.zeros((rows_of.shape[0], COLS), F32)
        for begin, size, field in segments(last, c):
            main = main + dot(rows_of[:, begin : begin + size], field)
        side = dot(rows_of, edge[...])
        tall = jnp.concatenate([side, main], axis=1)
        high = tall.astype(BF16)
        low = (tall - high.astype(F32)).astype(BF16)
        one = dot(high[:n_one], pone_in[...]) + dot(low[:n_one], pone_in[...])
        one_ref[c] = one.reshape(NZ // 2, ROWS // 2, COLS // 2)
        two = dot(high[n_one:], cols_of) + dot(low[n_one:], cols_of)
        two_ref[c] = two.reshape(NZ // 4, ROWS // 4, COLS // 4)

    for copy in info_copies():
        copy.wait_send()

    @pl.loop(0, CH)
    def _(c):
        for copy in [lower_copy(c), *join_copies(c)]:
            copy.wait_send()

        @pl.when(odd)
        def _():
            for hop in range(3):
                relay_copy(c, hop).wait_send()

        @pl.when(jnp.logical_not(odd))
        def _():
            far_copy(c).wait_send()

        @pl.loop(0, last)
        def _(s):
            for copy in row_copies(s, c) + edge_copies(s, c):
                copy.wait_send()

        for copy in row_copies(last, c, EDGE // 2) + edge_copies(last, c, EDGE // 2):
            copy.wait_send()


def _settle(*refs):
    sem = refs[-1]
    pairs = [(refs[0].at[c, z], refs[3].at[c, z]) for c in range(CH) for z in (pl.ds(0, 4), pl.ds(4, 4))]
    pairs += [(refs[1], refs[4]), (refs[2], refs[5])]
    copies = [pltpu.make_async_copy(src, dst, sem.at[n]) for n, (src, dst) in enumerate(pairs)]
    for copy in copies:
        copy.start()
    for copy in copies:
        copy.wait()


def solution(mesh):

    sizes = (mesh.shape["gx"], mesh.shape["gy"])
    prow = _pyramid_rows()
    pone, ptwo = _pyramid_cols()
    vmem = pl.BlockSpec(memory_space=pltpu.VMEM)
    hbm = pl.BlockSpec(memory_space=pltpu.HBM)
    dma = pltpu.SemaphoreType.DMA

    def per_device(tiles, offsets, psf):
        outs = pl.pallas_call(
            functools.partial(_kernel, sizes),
            out_shape=(
                pltpu.VMEM((CH, NZ, ROWS, COLS), F32),
                pltpu.VMEM((CH, NZ // 2, ROWS // 2, COLS // 2), F32),
                pltpu.VMEM((CH, NZ // 4, ROWS // 4, COLS // 4), F32),
            ),
            in_specs=[hbm, hbm, hbm, hbm, hbm, hbm],
            out_specs=(vmem, vmem, vmem),
            scratch_shapes=[
                pltpu.SMEM((1, 1, 2), jnp.int32),
                pltpu.SMEM((CH, 3, TAPS), F32),
                pltpu.VMEM((CH, NZ, TROWS, TCOLS), BF16),
                pltpu.VMEM(prow.shape, BF16),
                pltpu.VMEM(pone.shape, BF16),
                pltpu.VMEM(ptwo.shape, BF16),
                pltpu.VMEM((NZ * TROWS, COLS + LANES), BF16),
                pltpu.VMEM((CH, NZ, ROWS, COLS), BF16),
                pltpu.VMEM((CH, NZ, ROWS, COLS), BF16),
                pltpu.VMEM((CH, NZ, ROWS, COLS), BF16),
                pltpu.VMEM((CH, 2, NZ // 2, ROWS, LANES), BF16),
                pltpu.VMEM((CH, 2, NZ // 2, ROWS, LANES), BF16),
                pltpu.VMEM((16, LANES), F32),
                pltpu.VMEM((3, 16, LANES), F32),
                pltpu.VMEM((ROWS, COLS), F32),
                pltpu.VMEM((CH, NZ, ROWS, COLS), F32),
                pltpu.VMEM((STEPS, CH, NZ, ROWS, COLS), BF16),
                pltpu.VMEM((STEPS, CH, 2, NZ, EDGE, COLS), BF16),
                pltpu.VMEM((STEPS, CH, ROWS, LANES), BF16),
                pltpu.VMEM((STEPS, CH, ROWS, LANES), BF16),
                pltpu.VMEM((STEPS, CH, ROWS + 2 * EDGE, LANES), BF16),
                pltpu.VMEM((STEPS, CH, ROWS + 2 * EDGE, LANES), BF16),
                pltpu.VMEM((ALL, LANES), BF16),
                pltpu.VMEM((ALL, COLS), BF16),
                pltpu.VMEM((2, CH, COLS, COLS // 2), BF16),
                pltpu.VMEM((2, CH, OWN, ALL), BF16),
                dma((CH + 5,)),
                dma((CH, 3)),
                dma((CH, 3)),
                pltpu.VMEM((CH, 2, RELAY, ROWS, COLS), BF16),
                dma((CH, 3)),
                dma((CH, 3)),
                dma((3,)),
                dma((3,)),
                dma((STEPS, CH, 8)),
                dma((STEPS, CH, 8)),
            ],
            compiler_params=pltpu.CompilerParams(
                collective_id=0, has_side_effects=True, vmem_limit_bytes=48 * 1024 * 1024
            ),
        )(*[
            pltpu.with_memory_space_constraint(x, pltpu.HBM)
            for x in (offsets, psf, tiles, jnp.asarray(prow), jnp.asarray(pone), jnp.asarray(ptwo))
        ])
        return pl.pallas_call(
            _settle,
            out_shape=tuple(jax.ShapeDtypeStruct(o.shape, o.dtype) for o in outs),
            in_specs=[vmem] * 3,
            out_specs=(hbm,) * 3,
            scratch_shapes=[dma((2 * CH + 2,))],
            compiler_params=pltpu.CompilerParams(vmem_limit_bytes=4 * 1024 * 1024),
        )(*[pltpu.with_memory_space_constraint(o, pltpu.VMEM) for o in outs])

    in_specs = (P(None, None, "gy", "gx"), P("gy", "gx", None), P())
    out_specs = (P(None, None, "gy", "gx"),) * 3
    return jax.shard_map(
        per_device, mesh=mesh, in_specs=in_specs, out_specs=out_specs, check_vma=False
    )
```

```python
import functools

import jax
import jax.numpy as jnp
import numpy as np
from jax import lax
from jax.experimental import pallas as pl
from jax.experimental.pallas import tpu as pltpu
from jax.sharding import PartitionSpec as P

MESH = pl.DeviceIdType.MESH
F32 = jnp.float32
BF16 = jnp.bfloat16

CH, NZ, ROWS, COLS = 3, 8, 64, 512
MARGIN = 32
TROWS, TCOLS = ROWS + MARGIN, COLS + MARGIN
TAPS, HALF = 31, 15
ITERS = 2
STEPS = 2 * ITERS + 1
EDGE = 16
RELAY = 2
LANES = 128
OWN, STRIP = NZ * ROWS, NZ * EDGE
ALL = OWN + 2 * STRIP

GAUSS = np.array([1.0, 4.0, 6.0, 4.0, 1.0]) / 16.0


def _shrink(size_out, inputs):
    tap = np.asarray(inputs)[None, :] - 2 * np.arange(size_out)[:, None] + 2
    return np.where((tap >= 0) & (tap < 5), GAUSS[np.clip(tap, 0, 4)], 0.0)


def _shrink_twice(size_out, inputs, low_edge, high_edge):
    mid = np.arange(-2, 2 * size_out + 1)
    first = np.asarray(inputs)[None, :] - 2 * mid[:, None] + 2
    first = np.where((first >= 0) & (first < 5), GAUSS[np.clip(first, 0, 4)], 0.0)
    second = mid[None, :] - 2 * np.arange(size_out)[:, None] + 2
    second = np.where((second >= 0) & (second < 5), GAUSS[np.clip(second, 0, 4)], 0.0)
    keep = np.ones(mid.size)
    if low_edge:
        keep[mid < 0] = 0.0
    if high_edge:
        keep[mid >= 2 * size_out] = 0.0
    return second @ (keep[:, None] * first)


def _pyramid_rows():
    z_in = np.arange(NZ)
    z_one = _shrink(NZ // 2, z_in)
    z_two = _shrink(NZ // 4, np.arange(NZ // 2)) @ z_one
    parts = []
    for low, high in ((False, False), (True, False), (False, True)):
        blocks = []
        for coords, live in (
            (np.arange(ROWS), True),
            (np.arange(-EDGE, 0), not low),
            (np.arange(ROWS, ROWS + EDGE), not high),
        ):
            one = _shrink(ROWS // 2, coords) * live
            two = _shrink_twice(ROWS // 4, coords, low, high) * live
            blocks.append(np.concatenate([np.kron(z_one, one), np.kron(z_two, two)], axis=0))
        parts.append(np.concatenate(blocks, axis=1))
    return np.stack(parts).astype(jnp.bfloat16)


def _pyramid_cols():
    lane = np.arange(LANES)
    far = 10 * COLS
    edge = np.where(lane >= LANES - EDGE, lane - LANES, np.where(lane < EDGE, COLS + lane, far))
    coords = np.concatenate([edge, np.arange(COLS)])
    one = _shrink(COLS // 2, coords).T
    twos = [
        _shrink_twice(COLS // 4, coords, low, high).T
        for low, high in ((False, False), (True, False), (False, True))
    ]
    return one.astype(jnp.bfloat16), np.stack(twos).astype(jnp.bfloat16)


def _iota(shape, dim):
    return lax.broadcasted_iota(jnp.int32, shape, dim)


def _kernel(
    sizes,
    offsets_in,
    psf_in,
    tiles_ref,
    prow_ref,
    pone_ref,
    ptwo_ref,
    est_ref,
    one_ref,
    two_ref,
    offsets_ref,
    psf_ref,
    tiles_in,
    prow_in,
    pone_in,
    ptwo_in,
    shifted,
    own,
    low_send,
    low_recv,
    side_send,
    side_recv,
    info_send,
    info_recv,
    recip,
    joined,
    cur,
    strip_recv,
    pack_right,
    pack_left,
    left_recv,
    right_recv,
    edge,
    spread,
    mat_x,
    mat_zy,
    load_sem,
    join_send_sem,
    join_recv_sem,
    relay,
    relay_send_sem,
    relay_recv_sem,
    info_send_sem,
    info_recv_sem,
    send_sem,
    recv_sem,
):
    n_gx, n_gy = sizes
    gx, gy = lax.axis_index("gx"), lax.axis_index("gy")
    east, west = lax.rem(gx + 1, n_gx), lax.rem(gx + n_gx - 1, n_gx)
    south, north = lax.rem(gy + 1, n_gy), lax.rem(gy + n_gy - 1, n_gy)

    def at(x, y):
        return {"gx": x, "gy": y}

    around = [
        at(east, gy),
        at(west, gy),
        at(gx, south),
        at(gx, north),
        at(east, south),
        at(east, north),
        at(west, south),
        at(west, north),
    ]
    odd = lax.rem(gy, 2) == 1
    ring = [at(gx, lax.rem(gy + k, n_gy)) for k in (n_gy - 2, n_gy - 3, 2, 3)]
    barrier = pltpu.get_barrier_semaphore()
    for place in around + ring:
        pl.semaphore_signal(barrier, inc=1, device_id=place, device_id_type=MESH)

    tile_loads = [
        pltpu.make_async_copy(tiles_ref.at[c], tiles_in.at[c], load_sem.at[c]) for c in range(CH)
    ]
    constant_loads = [
        pltpu.make_async_copy(src, dst, load_sem.at[CH + n])
        for n, (src, dst) in enumerate(
            ((prow_ref, prow_in), (pone_ref, pone_in), (ptwo_ref, ptwo_in))
        )
    ]
    offsets_load = pltpu.make_async_copy(offsets_in, offsets_ref, load_sem.at[CH + 3])
    psf_load = pltpu.make_async_copy(psf_in, psf_ref, load_sem.at[CH + 4])
    for copy in [offsets_load, *tile_loads, psf_load, *constant_loads]:
        copy.start()

    def remote(src, dst, send, recv, place):
        return pltpu.make_async_remote_copy(
            src_ref=src, dst_ref=dst, send_sem=send, recv_sem=recv, device_id=place, device_id_type=MESH
        )

    def join_copies(c):
        return [
            remote(side_send.at[c, 0], side_recv.at[c, 0], join_send_sem.at[c, 1], join_recv_sem.at[c, 1], around[0]),
            remote(side_send.at[c, 1], side_recv.at[c, 1], join_send_sem.at[c, 2], join_recv_sem.at[c, 2], around[4]),
        ]

    def lower_copy(c, planes=slice(0, NZ - RELAY)):
        z = pl.ds(planes.start, planes.stop - planes.start)
        return remote(
            low_send.at[c, z], low_recv.at[c, z], join_send_sem.at[c, 0], join_recv_sem.at[c, 0], around[2]
        )

    far = pl.ds(NZ - RELAY, RELAY)

    def far_copy(c):
        return remote(
            low_send.at[c, far], low_recv.at[c, far], relay_send_sem.at[c, 0], relay_recv_sem.at[c, 0], around[2]
        )

    def relay_copy(c, hop):
        src = low_send.at[c, far] if hop == 0 else relay.at[c, hop - 1]
        dst = low_recv.at[c, far] if hop == 2 else relay.at[c, hop]
        return remote(
            src,
            dst,
            relay_send_sem.at[c, hop],
            relay_recv_sem.at[c, 0 if hop == 2 else hop + 1],
            ring[1] if hop == 2 else ring[0],
        )

    def info_copies():
        return [
            remote(info_send, info_recv.at[n], info_send_sem.at[n], info_recv_sem.at[n], around[k])
            for n, k in enumerate((0, 2, 4))
        ]

    def row_copies(s, c, rows=EDGE):
        parts = [
            (pl.ds(ROWS - rows, rows), 0, pl.ds(EDGE - rows, rows), around[2]),
            (pl.ds(0, rows), 1, pl.ds(0, rows), around[3]),
        ]
        return [
            remote(
                cur.at[s, c, :, src],
                strip_recv.at[s, c, n, :, dst],
                send_sem.at[s, c, n],
                recv_sem.at[s, c, n],
                place,
            )
            for src, n, dst, place in parts
        ]

    def edge_copies(s, c, rows=EDGE):
        first, last, main = pl.ds(0, rows), pl.ds(ROWS - rows, rows), pl.ds(0, ROWS)
        upper, lower = pl.ds(ROWS + EDGE - rows, rows), pl.ds(ROWS + EDGE, rows)
        right, left = pack_right.at[s, c], pack_left.at[s, c]
        parts = [
            (pack_right.at[s, c, last], left_recv.at[s, c, upper], around[4]),
            (pack_right.at[s, c, first], left_recv.at[s, c, lower], around[5]),
            (pack_left.at[s, c, last], right_recv.at[s, c, upper], around[6]),
            (pack_left.at[s, c, first], right_recv.at[s, c, lower], around[7]),
            (right, left_recv.at[s, c, main], around[0]),
            (left, right_recv.at[s, c, main], around[1]),
        ]
        return [
            remote(src, dst, send_sem.at[s, c, 2 + n], recv_sem.at[s, c, 2 + n], place)
            for n, (src, dst, place) in enumerate(parts)
        ]

    def start(copies):
        for copy in copies:
            copy.start()

    offsets_load.wait()
    top = offsets_ref[0, 0, 0]
    left = offsets_ref[0, 0, 1]
    info_send[0:8] = jnp.full((8, LANES), top.astype(F32), F32)
    info_send[8:16] = jnp.full((8, LANES), left.astype(F32), F32)

    def one_hot(cond):
        return jnp.where(cond, 1.0, 0.0).astype(BF16)

    half = COLS // 2
    shift_a = one_hot(_iota((half, half), 1) - _iota((half, half), 0) == left)
    shift_b = one_hot(_iota((384, half), 1) - _iota((384, half), 0) + LANES == left)
    shift_c = one_hot(_iota((160, LANES), 1) - _iota((160, LANES), 0) + LANES == left)
    row, col = _iota((4 * ROWS, 2 * TROWS), 0), _iota((4 * ROWS, 2 * TROWS), 1)
    row_odd = lax.rem(row, 2 * ROWS) >= ROWS
    col_odd = col >= TROWS
    row_at = lax.rem(row, ROWS) + jnp.where(row >= 2 * ROWS, ROWS, 0)
    col_at = col - jnp.where(col_odd, TROWS, 0)
    lower_it = one_hot((row_odd == col_odd) & (row_at - col_at == top))

    def dot(a, b):
        return jnp.dot(a, b, preferred_element_type=F32)

    unused = jnp.zeros((CH, NZ, EDGE // 2, COLS), BF16)
    strip_recv[STEPS - 1, :, 0, :, : EDGE // 2] = unused
    strip_recv[STEPS - 1, :, 1, :, EDGE // 2 :] = unused
    unused = jnp.zeros((CH, EDGE // 2, LANES), BF16)
    for side_recv_ref in (left_recv, right_recv):
        side_recv_ref[STEPS - 1, :, ROWS : ROWS + EDGE // 2] = unused
        side_recv_ref[STEPS - 1, :, ROWS + EDGE + EDGE // 2 :] = unused


    pairs = (NZ // 2 - 1, *range(NZ // 2 - 1))

    def place_tile(c, then):
        pltpu.make_async_copy(tiles_ref.at[c], tiles_in.at[c], load_sem.at[c]).wait()
        tile = tiles_in[c].reshape(NZ * TROWS, TCOLS)
        shifted[:, 0:half] = dot(tile[:, 0:half], shift_a).astype(BF16)
        shifted[:, half:COLS] = dot(tile[:, LANES:COLS], shift_b).astype(BF16)
        shifted[:, COLS:] = dot(tile[:, COLS - LANES :], shift_c).astype(BF16)
        for p in pairs:
            placed = dot(lower_it, shifted[2 * p * TROWS : 2 * (p + 1) * TROWS, :])
            for zz in range(2):
                own[c, 2 * p + zz] = placed[zz * ROWS : (zz + 1) * ROWS, :COLS].astype(BF16)
                low_send[c, 2 * p + zz] = placed[(2 + zz) * ROWS : (3 + zz) * ROWS, :COLS].astype(BF16)
            for part in range(2):
                even = placed[2 * part * ROWS : (2 * part + 1) * ROWS, COLS:]
                second = placed[(2 * part + 1) * ROWS : (2 * part + 2) * ROWS, COLS:]
                side_send[c, part, p] = (even + pltpu.roll(second, 64, 1)).astype(BF16)
            then(p)

    def send_rows(c, p):
        if 2 * p < NZ - RELAY:
            lower_copy(c, slice(2 * p, 2 * p + 2)).start()
        else:

            @pl.when(odd)
            def _():
                relay_copy(c, 0).start()

            @pl.when(jnp.logical_not(odd))
            def _():
                far_copy(c).start()

    place_tile(0, lambda p: None)
    pl.semaphore_wait(barrier, len(around) + len(ring))
    start(info_copies())
    for p in pairs:
        send_rows(0, p)
    start(join_copies(0))

    @pl.loop(1, CH)
    def _(c):
        place_tile(c, lambda p: send_rows(c, p))
        start(join_copies(c))

    psf_load.wait()

    @pl.loop(0, CH)
    def _(c):
        def total(a):
            t = psf_ref[c, a, 0]
            for k in range(1, TAPS):
                t = t + psf_ref[c, a, k]
            return t

        inv_x = 1.0 / jnp.full((1, LANES), total(2), F32)
        inv_zy = 1.0 / jnp.full((1, LANES), total(0) * total(1), F32)

        def banded(axis, diff, ks=range(TAPS)):
            ahead = jnp.zeros(diff.shape, F32)
            back = jnp.zeros(diff.shape, F32)
            for k in ks:
                hit = diff == k
                ahead = jnp.where(hit, psf_ref[c, axis, k], ahead)
                back = jnp.where(hit, psf_ref[c, axis, TAPS - 1 - k], back)
            return ahead, back

        square = (LANES, LANES)
        across = _iota(square, 0) - _iota(square, 1)
        for a, shift in enumerate((-113, 15, 143)):
            for d, block in enumerate(banded(2, across + shift)):
                block = (block * inv_x).astype(BF16)
                mat_x[d, c, a * LANES : (a + 1) * LANES, 0:LANES] = block
                mat_x[d, c, (a + 1) * LANES : (a + 2) * LANES, LANES:] = block
        zero = jnp.zeros(square, BF16)
        for d in range(2):
            mat_x[d, c, 0:LANES, LANES:] = zero
            mat_x[d, c, 3 * LANES :, 0:LANES] = zero

        yo = _iota((ROWS, LANES), 0)
        lane = _iota((ROWS, LANES), 1)
        inner = banded(1, lax.rem(lane, ROWS) - yo + HALF)
        above = banded(1, lax.rem(lane, EDGE) - EDGE - yo + HALF)
        below = banded(1, lax.rem(lane, EDGE) + ROWS - yo + HALF)
        has_above = jnp.where(gy > 0, 1.0, 0.0).astype(F32)
        has_below = jnp.where(gy < n_gy - 1, 1.0, 0.0).astype(F32)
        zo = _iota((NZ, LANES), 0)
        zlane = _iota((NZ, LANES), 1)
        depth_taps = range(HALF - NZ + 1, HALF + NZ)
        depth_own = [
            banded(0, 2 * j + lax.div(zlane, ROWS) - zo + HALF, depth_taps) for j in range(4)
        ]
        depth_edge = banded(0, lax.div(zlane, EDGE) - zo + HALF, depth_taps)
        for d in range(2):
            y_own = inner[d] * inv_zy
            y_above = above[d] * inv_zy * has_above
            y_below = below[d] * inv_zy * has_below
            for z in range(NZ):
                at_rows = slice(z * ROWS, (z + 1) * ROWS)
                for j in range(4):
                    mat_zy[d, c, at_rows, j * LANES : (j + 1) * LANES] = (
                        y_own * depth_own[j][d][z : z + 1]
                    ).astype(BF16)
                mat_zy[d, c, at_rows, 4 * LANES : 5 * LANES] = (
                    y_above * depth_edge[d][z : z + 1]
                ).astype(BF16)
                mat_zy[d, c, at_rows, 5 * LANES :] = (y_below * depth_edge[d][z : z + 1]).astype(BF16)

        @pl.when(odd)
        def _():
            relay_copy(c, 0).wait_recv()
            relay_copy(c, 1).start()

    @pl.when(odd)
    def _():
        @pl.loop(0, CH)
        def _(c):
            relay_copy(c, 1).wait_recv()
            relay_copy(c, 2).start()

    for copy in info_copies():
        copy.wait_recv()
    has_west = jnp.where(gx > 0, 1.0, 0.0).astype(F32)
    has_north = jnp.where(gy > 0, 1.0, 0.0).astype(F32)
    r = _iota((ROWS, COLS), 0).astype(F32)
    x = _iota((ROWS, COLS), 1).astype(F32)

    def told(n):
        t = jnp.broadcast_to(info_recv[n, 0:1, 0:1], (ROWS, COLS))
        l = jnp.broadcast_to(info_recv[n, 8:9, 0:1], (ROWS, COLS))
        return t, l

    def covers(cond):
        return jnp.where(cond, 1.0, 0.0)

    count = covers((r >= top.astype(F32)) & (x >= left.astype(F32)))
    t, l = told(0)
    count = count + has_west * covers((r >= t) & (x < l + float(MARGIN)))
    t, l = told(1)
    count = count + has_north * covers((r < t + float(MARGIN)) & (x >= l))
    t, l = told(2)
    count = count + has_west * has_north * covers((r < t + float(MARGIN)) & (x < l + float(MARGIN)))
    recip[...] = 1.0 / count

    lane = _iota((ROWS, LANES), 1)

    def pack_edges(s, c, plane):
        right = jnp.zeros((ROWS, LANES), F32)
        left_side = jnp.zeros((ROWS, LANES), F32)
        for z in range(NZ):
            here = lax.div(lane, EDGE) == z
            field = plane(z)
            right = jnp.where(
                here, pltpu.roll(field[:, COLS - LANES :], (EDGE * z + EDGE) % LANES, 1), right
            )
            left_side = jnp.where(here, pltpu.roll(field[:, :LANES], EDGE * z, 1), left_side)
        pack_right[s, c] = right.astype(BF16)
        pack_left[s, c] = left_side.astype(BF16)

    @pl.loop(0, CH)
    def _(c):
        for copy in [lower_copy(c), far_copy(c), *join_copies(c)]:
            copy.wait_recv()
        for z in range(NZ):
            total = own[c, z].astype(F32) + has_north * low_recv[c, z].astype(F32)
            spill = has_west * (
                side_recv[c, 0, z // 2].astype(F32) + has_north * side_recv[c, 1, z // 2].astype(F32)
            )
            if z % 2:
                spill = pltpu.roll(spill, 64, 1)
            spill = jnp.where(lane < 64, spill, 0.0)
            total = jnp.concatenate([total[:, :LANES] + spill, total[:, LANES:]], axis=1)
            value = total * recip[...]
            joined[c, z] = value
            est_ref[c, z] = value
            cur[0, c, z] = value.astype(BF16)
        pack_edges(0, c, lambda z: joined[c, z])
        start(edge_copies(0, c))
        start(row_copies(0, c))

    wide_lane = _iota((ROWS + 2 * EDGE, LANES), 1)
    from_west = (wide_lane >= LANES - EDGE) & (gx > 0)
    from_east = (wide_lane < EDGE) & (gx < n_gx - 1)

    def unpack_edges(s, c):
        west_side = left_recv[s, c].astype(F32)
        east_side = right_recv[s, c].astype(F32)
        for z in range(NZ):
            tile = jnp.where(
                from_west,
                pltpu.roll(west_side, (2 * LANES - EDGE - EDGE * z) % LANES, 1),
                jnp.where(from_east, pltpu.roll(east_side, (LANES - EDGE * z) % LANES, 1), 0.0),
            ).astype(BF16)
            edge[z * ROWS : (z + 1) * ROWS] = tile[:ROWS]
            edge[OWN + z * EDGE : OWN + (z + 1) * EDGE] = tile[ROWS : ROWS + EDGE]
            edge[OWN + STRIP + z * EDGE : OWN + STRIP + (z + 1) * EDGE] = tile[ROWS + EDGE :]

    def segments(s, c):
        return (
            (0, OWN, cur[s, c].reshape(OWN, COLS)),
            (OWN, 2 * STRIP, strip_recv[s, c].reshape(2 * STRIP, COLS)),
        )

    def blur(d, s, c):
        unpack_edges(s, c)
        taps = mat_x[d, c]
        for begin, size, field in segments(s, c):
            side = edge[begin : begin + size]
            first = jnp.concatenate([side, field[:, : COLS - LANES]], axis=1)
            spread[begin : begin + size, :half] = dot(first, taps).astype(BF16)
            second = jnp.concatenate([field[:, LANES:], side], axis=1)
            spread[begin : begin + size, half:] = dot(second, taps).astype(BF16)

    last = STEPS - 1

    def iterate(it, d, final):
        s = 2 * it + d
        rows = EDGE // 2 if final else EDGE

        @pl.loop(0, CH)
        def _(c):
            for copy in row_copies(s, c) + edge_copies(s, c):
                copy.wait_recv()
            blur(d, s, c)
            seen = dot(mat_zy[d, c], spread[...]).reshape(NZ, ROWS, COLS)
            if d == 0:
                value = joined[c] / seen
            else:
                value = est_ref[c] * seen
                est_ref[c] = value
            cur[s + 1, c] = value.astype(BF16)
            pack_edges(s + 1, c, lambda z: cur[s + 1, c, z].astype(F32))
            start(edge_copies(s + 1, c, rows))
            start(row_copies(s + 1, c, rows))

    @pl.loop(0, ITERS - 1)
    def _(it):
        iterate(it, 0, False)
        iterate(it, 1, False)

    iterate(ITERS - 1, 0, False)
    iterate(ITERS - 1, 1, True)

    for copy in constant_loads:
        copy.wait()
    rows_of = jnp.where(gy == 0, prow_in[1], jnp.where(gy == n_gy - 1, prow_in[2], prow_in[0]))
    cols_of = jnp.where(gx == 0, ptwo_in[1], jnp.where(gx == n_gx - 1, ptwo_in[2], ptwo_in[0]))
    n_one = NZ * ROWS // 4

    @pl.loop(0, CH)
    def _(c):
        for copy in row_copies(last, c, EDGE // 2) + edge_copies(last, c, EDGE // 2):
            copy.wait_recv()
        unpack_edges(last, c)
        main = jnp.zeros((rows_of.shape[0], COLS), F32)
        for begin, size, field in segments(last, c):
            main = main + dot(rows_of[:, begin : begin + size], field)
        side = dot(rows_of, edge[...])
        tall = jnp.concatenate([side, main], axis=1)
        high = tall.astype(BF16)
        low = (tall - high.astype(F32)).astype(BF16)
        one = dot(high[:n_one], pone_in[...]) + dot(low[:n_one], pone_in[...])
        one_ref[c] = one.reshape(NZ // 2, ROWS // 2, COLS // 2)
        two = dot(high[n_one:], cols_of) + dot(low[n_one:], cols_of)
        two_ref[c] = two.reshape(NZ // 4, ROWS // 4, COLS // 4)

    for copy in info_copies():
        copy.wait_send()

    @pl.loop(0, CH)
    def _(c):
        for copy in [lower_copy(c), *join_copies(c)]:
            copy.wait_send()

        @pl.when(odd)
        def _():
            for hop in range(3):
                relay_copy(c, hop).wait_send()

        @pl.when(jnp.logical_not(odd))
        def _():
            far_copy(c).wait_send()

        @pl.loop(0, last)
        def _(s):
            for copy in row_copies(s, c) + edge_copies(s, c):
                copy.wait_send()

        for copy in row_copies(last, c, EDGE // 2) + edge_copies(last, c, EDGE // 2):
            copy.wait_send()


def _settle(*refs):
    sem = refs[-1]
    pairs = [(refs[0].at[c, z], refs[3].at[c, z]) for c in range(CH) for z in (pl.ds(0, 4), pl.ds(4, 4))]
    pairs += [(refs[1], refs[4]), (refs[2], refs[5])]
    copies = [pltpu.make_async_copy(src, dst, sem.at[n]) for n, (src, dst) in enumerate(pairs)]
    for copy in copies:
        copy.start()
    for copy in copies:
        copy.wait()


def solution(mesh):

    sizes = (mesh.shape["gx"], mesh.shape["gy"])
    prow = _pyramid_rows()
    pone, ptwo = _pyramid_cols()
    vmem = pl.BlockSpec(memory_space=pltpu.VMEM)
    hbm = pl.BlockSpec(memory_space=pltpu.HBM)
    dma = pltpu.SemaphoreType.DMA

    def per_device(tiles, offsets, psf):
        outs = pl.pallas_call(
            functools.partial(_kernel, sizes),
            out_shape=(
                pltpu.VMEM((CH, NZ, ROWS, COLS), F32),
                pltpu.VMEM((CH, NZ // 2, ROWS // 2, COLS // 2), F32),
                pltpu.VMEM((CH, NZ // 4, ROWS // 4, COLS // 4), F32),
            ),
            in_specs=[hbm, hbm, hbm, hbm, hbm, hbm],
            out_specs=(vmem, vmem, vmem),
            scratch_shapes=[
                pltpu.SMEM((1, 1, 2), jnp.int32),
                pltpu.SMEM((CH, 3, TAPS), F32),
                pltpu.VMEM((CH, NZ, TROWS, TCOLS), BF16),
                pltpu.VMEM(prow.shape, BF16),
                pltpu.VMEM(pone.shape, BF16),
                pltpu.VMEM(ptwo.shape, BF16),
                pltpu.VMEM((NZ * TROWS, COLS + LANES), BF16),
                pltpu.VMEM((CH, NZ, ROWS, COLS), BF16),
                pltpu.VMEM((CH, NZ, ROWS, COLS), BF16),
                pltpu.VMEM((CH, NZ, ROWS, COLS), BF16),
                pltpu.VMEM((CH, 2, NZ // 2, ROWS, LANES), BF16),
                pltpu.VMEM((CH, 2, NZ // 2, ROWS, LANES), BF16),
                pltpu.VMEM((16, LANES), F32),
                pltpu.VMEM((3, 16, LANES), F32),
                pltpu.VMEM((ROWS, COLS), F32),
                pltpu.VMEM((CH, NZ, ROWS, COLS), F32),
                pltpu.VMEM((STEPS, CH, NZ, ROWS, COLS), BF16),
                pltpu.VMEM((STEPS, CH, 2, NZ, EDGE, COLS), BF16),
                pltpu.VMEM((STEPS, CH, ROWS, LANES), BF16),
                pltpu.VMEM((STEPS, CH, ROWS, LANES), BF16),
                pltpu.VMEM((STEPS, CH, ROWS + 2 * EDGE, LANES), BF16),
                pltpu.VMEM((STEPS, CH, ROWS + 2 * EDGE, LANES), BF16),
                pltpu.VMEM((ALL, LANES), BF16),
                pltpu.VMEM((ALL, COLS), BF16),
                pltpu.VMEM((2, CH, COLS, COLS // 2), BF16),
                pltpu.VMEM((2, CH, OWN, ALL), BF16),
                dma((CH + 5,)),
                dma((CH, 3)),
                dma((CH, 3)),
                pltpu.VMEM((CH, 2, RELAY, ROWS, COLS), BF16),
                dma((CH, 3)),
                dma((CH, 3)),
                dma((3,)),
                dma((3,)),
                dma((STEPS, CH, 8)),
                dma((STEPS, CH, 8)),
            ],
            compiler_params=pltpu.CompilerParams(
                collective_id=0, has_side_effects=True, vmem_limit_bytes=48 * 1024 * 1024
            ),
        )(*[
            pltpu.with_memory_space_constraint(x, pltpu.HBM)
            for x in (offsets, psf, tiles, jnp.asarray(prow), jnp.asarray(pone), jnp.asarray(ptwo))
        ])
        return pl.pallas_call(
            _settle,
            out_shape=tuple(jax.ShapeDtypeStruct(o.shape, o.dtype) for o in outs),
            in_specs=[vmem] * 3,
            out_specs=(hbm,) * 3,
            scratch_shapes=[dma((2 * CH + 2,))],
            compiler_params=pltpu.CompilerParams(vmem_limit_bytes=4 * 1024 * 1024),
        )(*[pltpu.with_memory_space_constraint(o, pltpu.VMEM) for o in outs])

    in_specs = (P(None, None, "gy", "gx"), P("gy", "gx", None), P())
    out_specs = (P(None, None, "gy", "gx"),) * 3
    return jax.shard_map(
        per_device, mesh=mesh, in_specs=in_specs, out_specs=out_specs, check_vma=False
    )
```

```python
import functools

import jax
import jax.numpy as jnp
import numpy as np
from jax import lax
from jax.experimental import pallas as pl
from jax.experimental.pallas import tpu as pltpu
from jax.sharding import PartitionSpec as P

MESH = pl.DeviceIdType.MESH
F32 = jnp.float32
BF16 = jnp.bfloat16

CH, NZ, ROWS, COLS = 3, 8, 64, 512
MARGIN = 32
TROWS, TCOLS = ROWS + MARGIN, COLS + MARGIN
TAPS, HALF = 31, 15
ITERS = 2
STEPS = 2 * ITERS + 1
EDGE = 16
RELAY = 2
LANES = 128
OWN, STRIP = NZ * ROWS, NZ * EDGE
ALL = OWN + 2 * STRIP

GAUSS = np.array([1.0, 4.0, 6.0, 4.0, 1.0]) / 16.0


def _shrink(size_out, inputs):
    tap = np.asarray(inputs)[None, :] - 2 * np.arange(size_out)[:, None] + 2
    return np.where((tap >= 0) & (tap < 5), GAUSS[np.clip(tap, 0, 4)], 0.0)


def _shrink_twice(size_out, inputs, low_edge, high_edge):
    mid = np.arange(-2, 2 * size_out + 1)
    first = np.asarray(inputs)[None, :] - 2 * mid[:, None] + 2
    first = np.where((first >= 0) & (first < 5), GAUSS[np.clip(first, 0, 4)], 0.0)
    second = mid[None, :] - 2 * np.arange(size_out)[:, None] + 2
    second = np.where((second >= 0) & (second < 5), GAUSS[np.clip(second, 0, 4)], 0.0)
    keep = np.ones(mid.size)
    if low_edge:
        keep[mid < 0] = 0.0
    if high_edge:
        keep[mid >= 2 * size_out] = 0.0
    return second @ (keep[:, None] * first)


def _pyramid_rows():
    z_in = np.arange(NZ)
    z_one = _shrink(NZ // 2, z_in)
    z_two = _shrink(NZ // 4, np.arange(NZ // 2)) @ z_one
    parts = []
    for low, high in ((False, False), (True, False), (False, True)):
        blocks = []
        for coords, live in (
            (np.arange(ROWS), True),
            (np.arange(-EDGE, 0), not low),
            (np.arange(ROWS, ROWS + EDGE), not high),
        ):
            one = _shrink(ROWS // 2, coords) * live
            two = _shrink_twice(ROWS // 4, coords, low, high) * live
            blocks.append(np.concatenate([np.kron(z_one, one), np.kron(z_two, two)], axis=0))
        parts.append(np.concatenate(blocks, axis=1))
    return np.stack(parts).astype(jnp.bfloat16)


def _pyramid_cols():
    lane = np.arange(LANES)
    far = 10 * COLS
    edge = np.where(lane >= LANES - EDGE, lane - LANES, np.where(lane < EDGE, COLS + lane, far))
    coords = np.concatenate([edge, np.arange(COLS)])
    one = _shrink(COLS // 2, coords).T
    twos = [
        _shrink_twice(COLS // 4, coords, low, high).T
        for low, high in ((False, False), (True, False), (False, True))
    ]
    return one.astype(jnp.bfloat16), np.stack(twos).astype(jnp.bfloat16)


def _iota(shape, dim):
    return lax.broadcasted_iota(jnp.int32, shape, dim)


def _kernel(
    sizes,
    offsets_in,
    psf_in,
    tiles_ref,
    prow_ref,
    pone_ref,
    ptwo_ref,
    est_ref,
    one_ref,
    two_ref,
    offsets_ref,
    psf_ref,
    tiles_in,
    prow_in,
    pone_in,
    ptwo_in,
    shifted,
    own,
    low_send,
    low_recv,
    side_send,
    side_recv,
    info_send,
    info_recv,
    recip,
    joined,
    cur,
    strip_recv,
    pack_right,
    pack_left,
    left_recv,
    right_recv,
    edge,
    spread,
    mat_x,
    mat_zy,
    load_sem,
    join_send_sem,
    join_recv_sem,
    relay,
    relay_send_sem,
    relay_recv_sem,
    info_send_sem,
    info_recv_sem,
    send_sem,
    recv_sem,
):
    n_gx, n_gy = sizes
    gx, gy = lax.axis_index("gx"), lax.axis_index("gy")
    east, west = lax.rem(gx + 1, n_gx), lax.rem(gx + n_gx - 1, n_gx)
    south, north = lax.rem(gy + 1, n_gy), lax.rem(gy + n_gy - 1, n_gy)

    def at(x, y):
        return {"gx": x, "gy": y}

    around = [
        at(east, gy),
        at(west, gy),
        at(gx, south),
        at(gx, north),
        at(east, south),
        at(east, north),
        at(west, south),
        at(west, north),
    ]
    odd = lax.rem(gy, 2) == 1
    ring = [at(gx, lax.rem(gy + k, n_gy)) for k in (n_gy - 2, n_gy - 3, 2, 3)]
    barrier = pltpu.get_barrier_semaphore()
    for place in around + ring:
        pl.semaphore_signal(barrier, inc=1, device_id=place, device_id_type=MESH)

    tile_loads = [
        pltpu.make_async_copy(tiles_ref.at[c], tiles_in.at[c], load_sem.at[c]) for c in range(CH)
    ]
    constant_loads = [
        pltpu.make_async_copy(src, dst, load_sem.at[CH + n])
        for n, (src, dst) in enumerate(
            ((prow_ref, prow_in), (pone_ref, pone_in), (ptwo_ref, ptwo_in))
        )
    ]
    offsets_load = pltpu.make_async_copy(offsets_in, offsets_ref, load_sem.at[CH + 3])
    psf_load = pltpu.make_async_copy(psf_in, psf_ref, load_sem.at[CH + 4])
    for copy in [offsets_load, *tile_loads, psf_load, *constant_loads]:
        copy.start()

    def remote(src, dst, send, recv, place):
        return pltpu.make_async_remote_copy(
            src_ref=src, dst_ref=dst, send_sem=send, recv_sem=recv, device_id=place, device_id_type=MESH
        )

    def join_copies(c):
        return [
            remote(side_send.at[c, 0], side_recv.at[c, 0], join_send_sem.at[c, 1], join_recv_sem.at[c, 1], around[0]),
            remote(side_send.at[c, 1], side_recv.at[c, 1], join_send_sem.at[c, 2], join_recv_sem.at[c, 2], around[4]),
        ]

    def lower_copy(c, planes=slice(0, NZ - RELAY)):
        z = pl.ds(planes.start, planes.stop - planes.start)
        return remote(
            low_send.at[c, z], low_recv.at[c, z], join_send_sem.at[c, 0], join_recv_sem.at[c, 0], around[2]
        )

    far = pl.ds(NZ - RELAY, RELAY)

    def far_copy(c):
        return remote(
            low_send.at[c, far], low_recv.at[c, far], relay_send_sem.at[c, 0], relay_recv_sem.at[c, 0], around[2]
        )

    def relay_copy(c, hop):
        src = low_send.at[c, far] if hop == 0 else relay.at[c, hop - 1]
        dst = low_recv.at[c, far] if hop == 2 else relay.at[c, hop]
        return remote(
            src,
            dst,
            relay_send_sem.at[c, hop],
            relay_recv_sem.at[c, 0 if hop == 2 else hop + 1],
            ring[1] if hop == 2 else ring[0],
        )

    def info_copies():
        return [
            remote(info_send, info_recv.at[n], info_send_sem.at[n], info_recv_sem.at[n], around[k])
            for n, k in enumerate((0, 2, 4))
        ]

    def row_copies(s, c, rows=EDGE):
        parts = [
            (pl.ds(ROWS - rows, rows), 0, pl.ds(EDGE - rows, rows), around[2]),
            (pl.ds(0, rows), 1, pl.ds(0, rows), around[3]),
        ]
        return [
            remote(
                cur.at[s, c, :, src],
                strip_recv.at[s, c, n, :, dst],
                send_sem.at[c, n],
                recv_sem.at[s % 2, c, n],
                place,
            )
            for src, n, dst, place in parts
        ]

    def edge_copies(s, c, rows=EDGE):
        first, last, main = pl.ds(0, rows), pl.ds(ROWS - rows, rows), pl.ds(0, ROWS)
        upper, lower = pl.ds(ROWS + EDGE - rows, rows), pl.ds(ROWS + EDGE, rows)
        right, left = pack_right.at[s, c], pack_left.at[s, c]
        parts = [
            (pack_right.at[s, c, last], left_recv.at[s, c, upper], around[4]),
            (pack_right.at[s, c, first], left_recv.at[s, c, lower], around[5]),
            (pack_left.at[s, c, last], right_recv.at[s, c, upper], around[6]),
            (pack_left.at[s, c, first], right_recv.at[s, c, lower], around[7]),
            (right, left_recv.at[s, c, main], around[0]),
            (left, right_recv.at[s, c, main], around[1]),
        ]
        return [
            remote(src, dst, send_sem.at[c, 2 + n], recv_sem.at[s % 2, c, 2 + n], place)
            for n, (src, dst, place) in enumerate(parts)
        ]

    def start(copies):
        for copy in copies:
            copy.start()

    offsets_load.wait()
    top = offsets_ref[0, 0, 0]
    left = offsets_ref[0, 0, 1]
    info_send[0:8] = jnp.full((8, LANES), top.astype(F32), F32)
    info_send[8:16] = jnp.full((8, LANES), left.astype(F32), F32)

    def one_hot(cond):
        return jnp.where(cond, 1.0, 0.0).astype(BF16)

    half = COLS // 2
    shift_a = one_hot(_iota((half, half), 1) - _iota((half, half), 0) == left)
    shift_b = one_hot(_iota((384, half), 1) - _iota((384, half), 0) + LANES == left)
    shift_c = one_hot(_iota((160, LANES), 1) - _iota((160, LANES), 0) + LANES == left)
    row, col = _iota((4 * ROWS, 2 * TROWS), 0), _iota((4 * ROWS, 2 * TROWS), 1)
    row_odd = lax.rem(row, 2 * ROWS) >= ROWS
    col_odd = col >= TROWS
    row_at = lax.rem(row, ROWS) + jnp.where(row >= 2 * ROWS, ROWS, 0)
    col_at = col - jnp.where(col_odd, TROWS, 0)
    lower_it = one_hot((row_odd == col_odd) & (row_at - col_at == top))

    def dot(a, b):
        return jnp.dot(a, b, preferred_element_type=F32)

    unused = jnp.zeros((CH, NZ, EDGE // 2, COLS), BF16)
    strip_recv[STEPS - 1, :, 0, :, : EDGE // 2] = unused
    strip_recv[STEPS - 1, :, 1, :, EDGE // 2 :] = unused
    unused = jnp.zeros((CH, EDGE // 2, LANES), BF16)
    for side_recv_ref in (left_recv, right_recv):
        side_recv_ref[STEPS - 1, :, ROWS : ROWS + EDGE // 2] = unused
        side_recv_ref[STEPS - 1, :, ROWS + EDGE + EDGE // 2 :] = unused


    pairs = (NZ // 2 - 1, *range(NZ // 2 - 1))

    def place_tile(c, then):
        pltpu.make_async_copy(tiles_ref.at[c], tiles_in.at[c], load_sem.at[c]).wait()
        tile = tiles_in[c].reshape(NZ * TROWS, TCOLS)
        shifted[:, 0:half] = dot(tile[:, 0:half], shift_a).astype(BF16)
        shifted[:, half:COLS] = dot(tile[:, LANES:COLS], shift_b).astype(BF16)
        shifted[:, COLS:] = dot(tile[:, COLS - LANES :], shift_c).astype(BF16)
        for p in pairs:
            placed = dot(lower_it, shifted[2 * p * TROWS : 2 * (p + 1) * TROWS, :])
            for zz in range(2):
                own[c, 2 * p + zz] = placed[zz * ROWS : (zz + 1) * ROWS, :COLS].astype(BF16)
                low_send[c, 2 * p + zz] = placed[(2 + zz) * ROWS : (3 + zz) * ROWS, :COLS].astype(BF16)
            for part in range(2):
                even = placed[2 * part * ROWS : (2 * part + 1) * ROWS, COLS:]
                second = placed[(2 * part + 1) * ROWS : (2 * part + 2) * ROWS, COLS:]
                side_send[c, part, p] = (even + pltpu.roll(second, 64, 1)).astype(BF16)
            then(p)

    def send_rows(c, p):
        if 2 * p < NZ - RELAY:
            lower_copy(c, slice(2 * p, 2 * p + 2)).start()
        else:

            @pl.when(odd)
            def _():
                relay_copy(c, 0).start()

            @pl.when(jnp.logical_not(odd))
            def _():
                far_copy(c).start()

    place_tile(0, lambda p: None)
    pl.semaphore_wait(barrier, len(around) + len(ring))
    start(info_copies())
    for p in pairs:
        send_rows(0, p)
    start(join_copies(0))

    @pl.loop(1, CH)
    def _(c):
        place_tile(c, lambda p: send_rows(c, p))
        start(join_copies(c))

    psf_load.wait()

    @pl.loop(0, CH)
    def _(c):
        def total(a):
            t = psf_ref[c, a, 0]
            for k in range(1, TAPS):
                t = t + psf_ref[c, a, k]
            return t

        inv_x = 1.0 / jnp.full((1, LANES), total(2), F32)
        inv_zy = 1.0 / jnp.full((1, LANES), total(0) * total(1), F32)

        def banded(axis, diff, ks=range(TAPS)):
            ahead = jnp.zeros(diff.shape, F32)
            back = jnp.zeros(diff.shape, F32)
            for k in ks:
                hit = diff == k
                ahead = jnp.where(hit, psf_ref[c, axis, k], ahead)
                back = jnp.where(hit, psf_ref[c, axis, TAPS - 1 - k], back)
            return ahead, back

        square = (LANES, LANES)
        across = _iota(square, 0) - _iota(square, 1)
        for a, shift in enumerate((-113, 15, 143)):
            for d, block in enumerate(banded(2, across + shift)):
                block = (block * inv_x).astype(BF16)
                mat_x[d, c, a * LANES : (a + 1) * LANES, 0:LANES] = block
                mat_x[d, c, (a + 1) * LANES : (a + 2) * LANES, LANES:] = block
        zero = jnp.zeros(square, BF16)
        for d in range(2):
            mat_x[d, c, 0:LANES, LANES:] = zero
            mat_x[d, c, 3 * LANES :, 0:LANES] = zero

        yo = _iota((ROWS, LANES), 0)
        lane = _iota((ROWS, LANES), 1)
        inner = banded(1, lax.rem(lane, ROWS) - yo + HALF)
        above = banded(1, lax.rem(lane, EDGE) - EDGE - yo + HALF)
        below = banded(1, lax.rem(lane, EDGE) + ROWS - yo + HALF)
        has_above = jnp.where(gy > 0, 1.0, 0.0).astype(F32)
        has_below = jnp.where(gy < n_gy - 1, 1.0, 0.0).astype(F32)
        zo = _iota((NZ, LANES), 0)
        zlane = _iota((NZ, LANES), 1)
        depth_taps = range(HALF - NZ + 1, HALF + NZ)
        depth_own = [
            banded(0, 2 * j + lax.div(zlane, ROWS) - zo + HALF, depth_taps) for j in range(4)
        ]
        depth_edge = banded(0, lax.div(zlane, EDGE) - zo + HALF, depth_taps)
        for d in range(2):
            y_own = inner[d] * inv_zy
            y_above = above[d] * inv_zy * has_above
            y_below = below[d] * inv_zy * has_below
            for z in range(NZ):
                at_rows = slice(z * ROWS, (z + 1) * ROWS)
                for j in range(4):
                    mat_zy[d, c, at_rows, j * LANES : (j + 1) * LANES] = (
                        y_own * depth_own[j][d][z : z + 1]
                    ).astype(BF16)
                mat_zy[d, c, at_rows, 4 * LANES : 5 * LANES] = (
                    y_above * depth_edge[d][z : z + 1]
                ).astype(BF16)
                mat_zy[d, c, at_rows, 5 * LANES :] = (y_below * depth_edge[d][z : z + 1]).astype(BF16)

        @pl.when(odd)
        def _():
            relay_copy(c, 0).wait_recv()
            relay_copy(c, 1).start()

    @pl.when(odd)
    def _():
        @pl.loop(0, CH)
        def _(c):
            relay_copy(c, 1).wait_recv()
            relay_copy(c, 2).start()

    for copy in info_copies():
        copy.wait_recv()
    has_west = jnp.where(gx > 0, 1.0, 0.0).astype(F32)
    has_north = jnp.where(gy > 0, 1.0, 0.0).astype(F32)
    r = _iota((ROWS, COLS), 0).astype(F32)
    x = _iota((ROWS, COLS), 1).astype(F32)

    def told(n):
        t = jnp.broadcast_to(info_recv[n, 0:1, 0:1], (ROWS, COLS))
        l = jnp.broadcast_to(info_recv[n, 8:9, 0:1], (ROWS, COLS))
        return t, l

    def covers(cond):
        return jnp.where(cond, 1.0, 0.0)

    count = covers((r >= top.astype(F32)) & (x >= left.astype(F32)))
    t, l = told(0)
    count = count + has_west * covers((r >= t) & (x < l + float(MARGIN)))
    t, l = told(1)
    count = count + has_north * covers((r < t + float(MARGIN)) & (x >= l))
    t, l = told(2)
    count = count + has_west * has_north * covers((r < t + float(MARGIN)) & (x < l + float(MARGIN)))
    recip[...] = 1.0 / count

    lane = _iota((ROWS, LANES), 1)

    def pack_edges(s, c, plane):
        right = jnp.zeros((ROWS, LANES), F32)
        left_side = jnp.zeros((ROWS, LANES), F32)
        for z in range(NZ):
            here = lax.div(lane, EDGE) == z
            field = plane(z)
            right = jnp.where(
                here, pltpu.roll(field[:, COLS - LANES :], (EDGE * z + EDGE) % LANES, 1), right
            )
            left_side = jnp.where(here, pltpu.roll(field[:, :LANES], EDGE * z, 1), left_side)
        pack_right[s, c] = right.astype(BF16)
        pack_left[s, c] = left_side.astype(BF16)

    @pl.loop(0, CH)
    def _(c):
        for copy in [lower_copy(c), far_copy(c), *join_copies(c)]:
            copy.wait_recv()
        for z in range(NZ):
            total = own[c, z].astype(F32) + has_north * low_recv[c, z].astype(F32)
            spill = has_west * (
                side_recv[c, 0, z // 2].astype(F32) + has_north * side_recv[c, 1, z // 2].astype(F32)
            )
            if z % 2:
                spill = pltpu.roll(spill, 64, 1)
            spill = jnp.where(lane < 64, spill, 0.0)
            total = jnp.concatenate([total[:, :LANES] + spill, total[:, LANES:]], axis=1)
            value = total * recip[...]
            joined[c, z] = value
            est_ref[c, z] = value
            cur[0, c, z] = value.astype(BF16)
        pack_edges(0, c, lambda z: joined[c, z])
        start(edge_copies(0, c))
        start(row_copies(0, c))

    wide_lane = _iota((ROWS + 2 * EDGE, LANES), 1)
    from_west = (wide_lane >= LANES - EDGE) & (gx > 0)
    from_east = (wide_lane < EDGE) & (gx < n_gx - 1)

    def unpack_edges(s, c):
        west_side = left_recv[s, c].astype(F32)
        east_side = right_recv[s, c].astype(F32)
        for z in range(NZ):
            tile = jnp.where(
                from_west,
                pltpu.roll(west_side, (2 * LANES - EDGE - EDGE * z) % LANES, 1),
                jnp.where(from_east, pltpu.roll(east_side, (LANES - EDGE * z) % LANES, 1), 0.0),
            ).astype(BF16)
            edge[z * ROWS : (z + 1) * ROWS] = tile[:ROWS]
            edge[OWN + z * EDGE : OWN + (z + 1) * EDGE] = tile[ROWS : ROWS + EDGE]
            edge[OWN + STRIP + z * EDGE : OWN + STRIP + (z + 1) * EDGE] = tile[ROWS + EDGE :]

    def segments(s, c):
        return (
            (0, OWN, cur[s, c].reshape(OWN, COLS)),
            (OWN, 2 * STRIP, strip_recv[s, c].reshape(2 * STRIP, COLS)),
        )

    def blur(d, s, c):
        unpack_edges(s, c)
        taps = mat_x[d, c]
        for begin, size, field in segments(s, c):
            side = edge[begin : begin + size]
            first = jnp.concatenate([side, field[:, : COLS - LANES]], axis=1)
            spread[begin : begin + size, :half] = dot(first, taps).astype(BF16)
            second = jnp.concatenate([field[:, LANES:], side], axis=1)
            spread[begin : begin + size, half:] = dot(second, taps).astype(BF16)

    last = STEPS - 1

    def iterate(it, d, final):
        s = 2 * it + d
        rows = EDGE // 2 if final else EDGE

        @pl.loop(0, CH)
        def _(c):
            for copy in row_copies(s, c) + edge_copies(s, c):
                copy.wait_recv()
            blur(d, s, c)
            seen = dot(mat_zy[d, c], spread[...]).reshape(NZ, ROWS, COLS)
            if d == 0:
                value = joined[c] / seen
            else:
                value = est_ref[c] * seen
                est_ref[c] = value
            cur[s + 1, c] = value.astype(BF16)
            pack_edges(s + 1, c, lambda z: cur[s + 1, c, z].astype(F32))
            for copy in edge_copies(s, c) + row_copies(s, c):
                copy.wait_send()
            start(edge_copies(s + 1, c, rows))
            start(row_copies(s + 1, c, rows))

    def join_sent():
        for copy in info_copies():
            copy.wait_send()

        @pl.loop(0, CH)
        def _(c):
            for copy in [lower_copy(c), *join_copies(c)]:
                copy.wait_send()

            @pl.when(odd)
            def _():
                for hop in range(3):
                    relay_copy(c, hop).wait_send()

            @pl.when(jnp.logical_not(odd))
            def _():
                far_copy(c).wait_send()

    for it in range(ITERS):
        iterate(it, 0, False)
        if it == 0:
            join_sent()
        iterate(it, 1, it == ITERS - 1)

    for copy in constant_loads:
        copy.wait()
    rows_of = jnp.where(gy == 0, prow_in[1], jnp.where(gy == n_gy - 1, prow_in[2], prow_in[0]))
    cols_of = jnp.where(gx == 0, ptwo_in[1], jnp.where(gx == n_gx - 1, ptwo_in[2], ptwo_in[0]))
    n_one = NZ * ROWS // 4

    @pl.loop(0, CH)
    def _(c):
        for copy in row_copies(last, c, EDGE // 2) + edge_copies(last, c, EDGE // 2):
            copy.wait_recv()
        unpack_edges(last, c)
        main = jnp.zeros((rows_of.shape[0], COLS), F32)
        for begin, size, field in segments(last, c):
            main = main + dot(rows_of[:, begin : begin + size], field)
        side = dot(rows_of, edge[...])
        tall = jnp.concatenate([side, main], axis=1)
        high = tall.astype(BF16)
        low = (tall - high.astype(F32)).astype(BF16)
        one = dot(high[:n_one], pone_in[...]) + dot(low[:n_one], pone_in[...])
        one_ref[c] = one.reshape(NZ // 2, ROWS // 2, COLS // 2)
        two = dot(high[n_one:], cols_of) + dot(low[n_one:], cols_of)
        two_ref[c] = two.reshape(NZ // 4, ROWS // 4, COLS // 4)
        for copy in row_copies(last, c, EDGE // 2) + edge_copies(last, c, EDGE // 2):
            copy.wait_send()

def _settle(*refs):
    sem = refs[-1]
    pairs = [(refs[0].at[c, z], refs[3].at[c, z]) for c in range(CH) for z in (pl.ds(0, 4), pl.ds(4, 4))]
    pairs += [(refs[1], refs[4]), (refs[2], refs[5])]
    copies = [pltpu.make_async_copy(src, dst, sem.at[n]) for n, (src, dst) in enumerate(pairs)]
    for copy in copies:
        copy.start()
    for copy in copies:
        copy.wait()


def solution(mesh):

    sizes = (mesh.shape["gx"], mesh.shape["gy"])
    prow = _pyramid_rows()
    pone, ptwo = _pyramid_cols()
    vmem = pl.BlockSpec(memory_space=pltpu.VMEM)
    hbm = pl.BlockSpec(memory_space=pltpu.HBM)
    dma = pltpu.SemaphoreType.DMA

    def per_device(tiles, offsets, psf):
        outs = pl.pallas_call(
            functools.partial(_kernel, sizes),
            out_shape=(
                pltpu.VMEM((CH, NZ, ROWS, COLS), F32),
                pltpu.VMEM((CH, NZ // 2, ROWS // 2, COLS // 2), F32),
                pltpu.VMEM((CH, NZ // 4, ROWS // 4, COLS // 4), F32),
            ),
            in_specs=[hbm, hbm, hbm, hbm, hbm, hbm],
            out_specs=(vmem, vmem, vmem),
            scratch_shapes=[
                pltpu.SMEM((1, 1, 2), jnp.int32),
                pltpu.SMEM((CH, 3, TAPS), F32),
                pltpu.VMEM((CH, NZ, TROWS, TCOLS), BF16),
                pltpu.VMEM(prow.shape, BF16),
                pltpu.VMEM(pone.shape, BF16),
                pltpu.VMEM(ptwo.shape, BF16),
                pltpu.VMEM((NZ * TROWS, COLS + LANES), BF16),
                pltpu.VMEM((CH, NZ, ROWS, COLS), BF16),
                pltpu.VMEM((CH, NZ, ROWS, COLS), BF16),
                pltpu.VMEM((CH, NZ, ROWS, COLS), BF16),
                pltpu.VMEM((CH, 2, NZ // 2, ROWS, LANES), BF16),
                pltpu.VMEM((CH, 2, NZ // 2, ROWS, LANES), BF16),
                pltpu.VMEM((16, LANES), F32),
                pltpu.VMEM((3, 16, LANES), F32),
                pltpu.VMEM((ROWS, COLS), F32),
                pltpu.VMEM((CH, NZ, ROWS, COLS), F32),
                pltpu.VMEM((STEPS, CH, NZ, ROWS, COLS), BF16),
                pltpu.VMEM((STEPS, CH, 2, NZ, EDGE, COLS), BF16),
                pltpu.VMEM((STEPS, CH, ROWS, LANES), BF16),
                pltpu.VMEM((STEPS, CH, ROWS, LANES), BF16),
                pltpu.VMEM((STEPS, CH, ROWS + 2 * EDGE, LANES), BF16),
                pltpu.VMEM((STEPS, CH, ROWS + 2 * EDGE, LANES), BF16),
                pltpu.VMEM((ALL, LANES), BF16),
                pltpu.VMEM((ALL, COLS), BF16),
                pltpu.VMEM((2, CH, COLS, COLS // 2), BF16),
                pltpu.VMEM((2, CH, OWN, ALL), BF16),
                dma((CH + 5,)),
                dma((CH, 3)),
                dma((CH, 3)),
                pltpu.VMEM((CH, 2, RELAY, ROWS, COLS), BF16),
                dma((CH, 3)),
                dma((CH, 3)),
                dma((3,)),
                dma((3,)),
                dma((CH, 8)),
                dma((2, CH, 8)),
            ],
            compiler_params=pltpu.CompilerParams(
                collective_id=0, has_side_effects=True, vmem_limit_bytes=48 * 1024 * 1024
            ),
        )(*[
            pltpu.with_memory_space_constraint(x, pltpu.HBM)
            for x in (offsets, psf, tiles, jnp.asarray(prow), jnp.asarray(pone), jnp.asarray(ptwo))
        ])
        return pl.pallas_call(
            _settle,
            out_shape=tuple(jax.ShapeDtypeStruct(o.shape, o.dtype) for o in outs),
            in_specs=[vmem] * 3,
            out_specs=(hbm,) * 3,
            scratch_shapes=[dma((2 * CH + 2,))],
            compiler_params=pltpu.CompilerParams(vmem_limit_bytes=4 * 1024 * 1024),
        )(*[pltpu.with_memory_space_constraint(o, pltpu.VMEM) for o in outs])

    in_specs = (P(None, None, "gy", "gx"), P("gy", "gx", None), P())
    out_specs = (P(None, None, "gy", "gx"),) * 3
    return jax.shard_map(
        per_device, mesh=mesh, in_specs=in_specs, out_specs=out_specs, check_vma=False
    )
```

```python
import functools

import jax
import jax.numpy as jnp
import numpy as np
from jax import lax
from jax.experimental import pallas as pl
from jax.experimental.pallas import tpu as pltpu
from jax.sharding import PartitionSpec as P

MESH = pl.DeviceIdType.MESH
F32 = jnp.float32
BF16 = jnp.bfloat16

CH, NZ, ROWS, COLS = 3, 8, 64, 512
MARGIN = 32
TROWS, TCOLS = ROWS + MARGIN, COLS + MARGIN
TAPS, HALF = 31, 15
ITERS = 2
STEPS = 2 * ITERS + 1
EDGE = 16
RELAY = 2
LANES = 128
OWN, STRIP = NZ * ROWS, NZ * EDGE
ALL = OWN + 2 * STRIP

GAUSS = np.array([1.0, 4.0, 6.0, 4.0, 1.0]) / 16.0


def _shrink(size_out, inputs):
    tap = np.asarray(inputs)[None, :] - 2 * np.arange(size_out)[:, None] + 2
    return np.where((tap >= 0) & (tap < 5), GAUSS[np.clip(tap, 0, 4)], 0.0)


def _shrink_twice(size_out, inputs, low_edge, high_edge):
    mid = np.arange(-2, 2 * size_out + 1)
    first = np.asarray(inputs)[None, :] - 2 * mid[:, None] + 2
    first = np.where((first >= 0) & (first < 5), GAUSS[np.clip(first, 0, 4)], 0.0)
    second = mid[None, :] - 2 * np.arange(size_out)[:, None] + 2
    second = np.where((second >= 0) & (second < 5), GAUSS[np.clip(second, 0, 4)], 0.0)
    keep = np.ones(mid.size)
    if low_edge:
        keep[mid < 0] = 0.0
    if high_edge:
        keep[mid >= 2 * size_out] = 0.0
    return second @ (keep[:, None] * first)


def _pyramid_rows():
    z_in = np.arange(NZ)
    z_one = _shrink(NZ // 2, z_in)
    z_two = _shrink(NZ // 4, np.arange(NZ // 2)) @ z_one
    parts = []
    for low, high in ((False, False), (True, False), (False, True)):
        blocks = []
        for coords, live in (
            (np.arange(ROWS), True),
            (np.arange(-EDGE, 0), not low),
            (np.arange(ROWS, ROWS + EDGE), not high),
        ):
            one = _shrink(ROWS // 2, coords) * live
            two = _shrink_twice(ROWS // 4, coords, low, high) * live
            blocks.append(np.concatenate([np.kron(z_one, one), np.kron(z_two, two)], axis=0))
        parts.append(np.concatenate(blocks, axis=1))
    return np.stack(parts).astype(jnp.bfloat16)


def _pyramid_cols():
    lane = np.arange(LANES)
    far = 10 * COLS
    edge = np.where(lane >= LANES - EDGE, lane - LANES, np.where(lane < EDGE, COLS + lane, far))
    coords = np.concatenate([edge, np.arange(COLS)])
    one = _shrink(COLS // 2, coords).T
    twos = [
        _shrink_twice(COLS // 4, coords, low, high).T
        for low, high in ((False, False), (True, False), (False, True))
    ]
    return one.astype(jnp.bfloat16), np.stack(twos).astype(jnp.bfloat16)


def _iota(shape, dim):
    return lax.broadcasted_iota(jnp.int32, shape, dim)


def _kernel(
    sizes,
    offsets_in,
    psf_in,
    tiles_ref,
    prow_ref,
    pone_ref,
    ptwo_ref,
    est_ref,
    one_ref,
    two_ref,
    offsets_ref,
    psf_ref,
    tiles_in,
    prow_in,
    pone_in,
    ptwo_in,
    shifted,
    own,
    low_send,
    low_recv,
    side_send,
    side_recv,
    info_send,
    info_recv,
    recip,
    joined,
    cur,
    strip_recv,
    pack_right,
    pack_left,
    left_recv,
    right_recv,
    edge,
    spread,
    mat_x,
    mat_zy,
    load_sem,
    join_send_sem,
    join_recv_sem,
    relay,
    relay_send_sem,
    relay_recv_sem,
    info_send_sem,
    info_recv_sem,
    send_sem,
    recv_sem,
):
    n_gx, n_gy = sizes
    gx, gy = lax.axis_index("gx"), lax.axis_index("gy")
    east, west = lax.rem(gx + 1, n_gx), lax.rem(gx + n_gx - 1, n_gx)
    south, north = lax.rem(gy + 1, n_gy), lax.rem(gy + n_gy - 1, n_gy)

    def at(x, y):
        return {"gx": x, "gy": y}

    around = [
        at(east, gy),
        at(west, gy),
        at(gx, south),
        at(gx, north),
        at(east, south),
        at(east, north),
        at(west, south),
        at(west, north),
    ]
    odd = lax.rem(gy, 2) == 1
    ring = [at(gx, lax.rem(gy + k, n_gy)) for k in (n_gy - 2, n_gy - 3, 2, 3)]
    barrier = pltpu.get_barrier_semaphore()
    for place in around + ring:
        pl.semaphore_signal(barrier, inc=1, device_id=place, device_id_type=MESH)

    tile_loads = [
        pltpu.make_async_copy(tiles_ref.at[c], tiles_in.at[c], load_sem.at[c]) for c in range(CH)
    ]
    constant_loads = [
        pltpu.make_async_copy(src, dst, load_sem.at[CH + n])
        for n, (src, dst) in enumerate(
            ((prow_ref, prow_in), (pone_ref, pone_in), (ptwo_ref, ptwo_in))
        )
    ]
    offsets_load = pltpu.make_async_copy(offsets_in, offsets_ref, load_sem.at[CH + 3])
    psf_load = pltpu.make_async_copy(psf_in, psf_ref, load_sem.at[CH + 4])
    offsets_load.start()
    tile_loads[0].start()

    def remote(src, dst, send, recv, place):
        return pltpu.make_async_remote_copy(
            src_ref=src, dst_ref=dst, send_sem=send, recv_sem=recv, device_id=place, device_id_type=MESH
        )

    def join_copies(c):
        return [
            remote(side_send.at[c, 0], side_recv.at[c, 0], join_send_sem.at[c, 1], join_recv_sem.at[c, 1], around[0]),
            remote(side_send.at[c, 1], side_recv.at[c, 1], join_send_sem.at[c, 2], join_recv_sem.at[c, 2], around[4]),
        ]

    def lower_copy(c, planes=slice(0, NZ - RELAY)):
        z = pl.ds(planes.start, planes.stop - planes.start)
        return remote(
            low_send.at[c, z], low_recv.at[c, z], join_send_sem.at[c, 0], join_recv_sem.at[c, 0], around[2]
        )

    far = pl.ds(NZ - RELAY, RELAY)

    def far_copy(c):
        return remote(
            low_send.at[c, far], low_recv.at[c, far], relay_send_sem.at[c, 0], relay_recv_sem.at[c, 0], around[2]
        )

    def relay_copy(c, hop):
        src = low_send.at[c, far] if hop == 0 else relay.at[c, hop - 1]
        dst = low_recv.at[c, far] if hop == 2 else relay.at[c, hop]
        return remote(
            src,
            dst,
            relay_send_sem.at[c, hop],
            relay_recv_sem.at[c, 0 if hop == 2 else hop + 1],
            ring[1] if hop == 2 else ring[0],
        )

    def info_copies():
        return [
            remote(info_send, info_recv.at[n], info_send_sem.at[n], info_recv_sem.at[n], around[k])
            for n, k in enumerate((0, 2, 4))
        ]

    def row_copies(s, c, rows=EDGE):
        parts = [
            (pl.ds(ROWS - rows, rows), 0, pl.ds(EDGE - rows, rows), around[2]),
            (pl.ds(0, rows), 1, pl.ds(0, rows), around[3]),
        ]
        return [
            remote(
                cur.at[s, c, :, src],
                strip_recv.at[s, c, n, :, dst],
                send_sem.at[c, n],
                recv_sem.at[s % 2, c, 0],
                place,
            )
            for src, n, dst, place in parts
        ]

    def edge_copies(s, c, rows=EDGE):
        first, last, main = pl.ds(0, rows), pl.ds(ROWS - rows, rows), pl.ds(0, ROWS)
        upper, lower = pl.ds(ROWS + EDGE - rows, rows), pl.ds(ROWS + EDGE, rows)
        right, left = pack_right.at[s, c], pack_left.at[s, c]
        parts = [
            (pack_right.at[s, c, last], left_recv.at[s, c, upper], around[4], 1),
            (pack_right.at[s, c, first], left_recv.at[s, c, lower], around[5], 1),
            (pack_left.at[s, c, last], right_recv.at[s, c, upper], around[6], 2),
            (pack_left.at[s, c, first], right_recv.at[s, c, lower], around[7], 2),
            (right, left_recv.at[s, c, main], around[0], 1),
            (left, right_recv.at[s, c, main], around[1], 2),
        ]
        return [
            remote(src, dst, send_sem.at[c, 2 + n], recv_sem.at[s % 2, c, side], place)
            for n, (src, dst, place, side) in enumerate(parts)
        ]

    def arrived(s, c, rows=EDGE):
        near, side = pl.ds(0, rows), pl.ds(0, ROWS + 2 * rows)
        for n, ref in enumerate(
            (strip_recv.at[s, c, :, :, near], left_recv.at[s, c, side], right_recv.at[s, c, side])
        ):
            remote(ref, ref, send_sem.at[c, n], recv_sem.at[s % 2, c, n], around[0]).wait_recv()

    def start(copies):
        for copy in copies:
            copy.start()

    offsets_load.wait()
    top = offsets_ref[0, 0, 0]
    left = offsets_ref[0, 0, 1]
    info_send[0:8] = jnp.full((8, LANES), top.astype(F32), F32)
    info_send[8:16] = jnp.full((8, LANES), left.astype(F32), F32)

    def one_hot(cond):
        return jnp.where(cond, 1.0, 0.0).astype(BF16)

    half = COLS // 2
    shift_a = one_hot(_iota((half, half), 1) - _iota((half, half), 0) == left)
    shift_b = one_hot(_iota((384, half), 1) - _iota((384, half), 0) + LANES == left)
    shift_c = one_hot(_iota((160, LANES), 1) - _iota((160, LANES), 0) + LANES == left)
    row, col = _iota((4 * ROWS, 2 * TROWS), 0), _iota((4 * ROWS, 2 * TROWS), 1)
    row_odd = lax.rem(row, 2 * ROWS) >= ROWS
    col_odd = col >= TROWS
    row_at = lax.rem(row, ROWS) + jnp.where(row >= 2 * ROWS, ROWS, 0)
    col_at = col - jnp.where(col_odd, TROWS, 0)
    lower_it = one_hot((row_odd == col_odd) & (row_at - col_at == top))

    def dot(a, b):
        return jnp.dot(a, b, preferred_element_type=F32)

    unused = jnp.zeros((CH, NZ, EDGE // 2, COLS), BF16)
    strip_recv[STEPS - 1, :, 0, :, : EDGE // 2] = unused
    strip_recv[STEPS - 1, :, 1, :, EDGE // 2 :] = unused
    unused = jnp.zeros((CH, EDGE // 2, LANES), BF16)
    for side_recv_ref in (left_recv, right_recv):
        side_recv_ref[STEPS - 1, :, ROWS : ROWS + EDGE // 2] = unused
        side_recv_ref[STEPS - 1, :, ROWS + EDGE + EDGE // 2 :] = unused


    pairs = (NZ // 2 - 1, *range(NZ // 2 - 1))

    def place_tile(c, then):
        pltpu.make_async_copy(tiles_ref.at[c], tiles_in.at[c], load_sem.at[c]).wait()
        tile = tiles_in[c].reshape(NZ * TROWS, TCOLS)
        shifted[:, 0:half] = dot(tile[:, 0:half], shift_a).astype(BF16)
        shifted[:, half:COLS] = dot(tile[:, LANES:COLS], shift_b).astype(BF16)
        shifted[:, COLS:] = dot(tile[:, COLS - LANES :], shift_c).astype(BF16)
        for p in pairs:
            placed = dot(lower_it, shifted[2 * p * TROWS : 2 * (p + 1) * TROWS, :])
            for zz in range(2):
                own[c, 2 * p + zz] = placed[zz * ROWS : (zz + 1) * ROWS, :COLS].astype(BF16)
                low_send[c, 2 * p + zz] = placed[(2 + zz) * ROWS : (3 + zz) * ROWS, :COLS].astype(BF16)
            for part in range(2):
                even = placed[2 * part * ROWS : (2 * part + 1) * ROWS, COLS:]
                second = placed[(2 * part + 1) * ROWS : (2 * part + 2) * ROWS, COLS:]
                side_send[c, part, p] = (even + pltpu.roll(second, 64, 1)).astype(BF16)
            then(p)

    def send_rows(c, p):
        if 2 * p < NZ - RELAY:
            lower_copy(c, slice(2 * p, 2 * p + 2)).start()
        else:

            @pl.when(odd)
            def _():
                relay_copy(c, 0).start()

            @pl.when(jnp.logical_not(odd))
            def _():
                far_copy(c).start()

    place_tile(0, lambda p: None)
    for copy in [*tile_loads[1:], psf_load, *constant_loads]:
        copy.start()
    pl.semaphore_wait(barrier, len(around) + len(ring))
    start(info_copies())
    for p in pairs:
        send_rows(0, p)
    start(join_copies(0))

    @pl.loop(1, CH)
    def _(c):
        place_tile(c, lambda p: send_rows(c, p))
        start(join_copies(c))

    psf_load.wait()

    @pl.loop(0, CH)
    def _(c):
        def total(a):
            t = psf_ref[c, a, 0]
            for k in range(1, TAPS):
                t = t + psf_ref[c, a, k]
            return t

        inv_x = 1.0 / jnp.full((1, LANES), total(2), F32)
        inv_zy = 1.0 / jnp.full((1, LANES), total(0) * total(1), F32)

        def banded(axis, diff, ks=range(TAPS)):
            ahead = jnp.zeros(diff.shape, F32)
            back = jnp.zeros(diff.shape, F32)
            for k in ks:
                hit = diff == k
                ahead = jnp.where(hit, psf_ref[c, axis, k], ahead)
                back = jnp.where(hit, psf_ref[c, axis, TAPS - 1 - k], back)
            return ahead, back

        square = (LANES, LANES)
        across = _iota(square, 0) - _iota(square, 1)
        for a, shift in enumerate((-113, 15, 143)):
            for d, block in enumerate(banded(2, across + shift)):
                block = (block * inv_x).astype(BF16)
                mat_x[d, c, a * LANES : (a + 1) * LANES, 0:LANES] = block
                mat_x[d, c, (a + 1) * LANES : (a + 2) * LANES, LANES:] = block
        zero = jnp.zeros(square, BF16)
        for d in range(2):
            mat_x[d, c, 0:LANES, LANES:] = zero
            mat_x[d, c, 3 * LANES :, 0:LANES] = zero

        yo = _iota((ROWS, LANES), 0)
        lane = _iota((ROWS, LANES), 1)
        inner = banded(1, lax.rem(lane, ROWS) - yo + HALF)
        above = banded(1, lax.rem(lane, EDGE) - EDGE - yo + HALF)
        below = banded(1, lax.rem(lane, EDGE) + ROWS - yo + HALF)
        has_above = jnp.where(gy > 0, 1.0, 0.0).astype(F32)
        has_below = jnp.where(gy < n_gy - 1, 1.0, 0.0).astype(F32)
        zo = _iota((NZ, LANES), 0)
        zlane = _iota((NZ, LANES), 1)
        depth_taps = range(HALF - NZ + 1, HALF + NZ)
        depth_own = [
            banded(0, 2 * j + lax.div(zlane, ROWS) - zo + HALF, depth_taps) for j in range(4)
        ]
        depth_edge = banded(0, lax.div(zlane, EDGE) - zo + HALF, depth_taps)
        for d in range(2):
            y_own = inner[d] * inv_zy
            y_above = above[d] * inv_zy * has_above
            y_below = below[d] * inv_zy * has_below
            for z in range(NZ):
                at_rows = slice(z * ROWS, (z + 1) * ROWS)
                for j in range(4):
                    mat_zy[d, c, at_rows, j * LANES : (j + 1) * LANES] = (
                        y_own * depth_own[j][d][z : z + 1]
                    ).astype(BF16)
                mat_zy[d, c, at_rows, 4 * LANES : 5 * LANES] = (
                    y_above * depth_edge[d][z : z + 1]
                ).astype(BF16)
                mat_zy[d, c, at_rows, 5 * LANES :] = (y_below * depth_edge[d][z : z + 1]).astype(BF16)

        @pl.when(odd)
        def _():
            relay_copy(c, 0).wait_recv()
            relay_copy(c, 1).start()

    @pl.when(odd)
    def _():
        @pl.loop(0, CH)
        def _(c):
            relay_copy(c, 1).wait_recv()
            relay_copy(c, 2).start()

    for copy in info_copies():
        copy.wait_recv()
    has_west = jnp.where(gx > 0, 1.0, 0.0).astype(F32)
    has_north = jnp.where(gy > 0, 1.0, 0.0).astype(F32)
    r = _iota((ROWS, COLS), 0).astype(F32)
    x = _iota((ROWS, COLS), 1).astype(F32)

    def told(n):
        t = jnp.broadcast_to(info_recv[n, 0:1, 0:1], (ROWS, COLS))
        l = jnp.broadcast_to(info_recv[n, 8:9, 0:1], (ROWS, COLS))
        return t, l

    def covers(cond):
        return jnp.where(cond, 1.0, 0.0)

    count = covers((r >= top.astype(F32)) & (x >= left.astype(F32)))
    t, l = told(0)
    count = count + has_west * covers((r >= t) & (x < l + float(MARGIN)))
    t, l = told(1)
    count = count + has_north * covers((r < t + float(MARGIN)) & (x >= l))
    t, l = told(2)
    count = count + has_west * has_north * covers((r < t + float(MARGIN)) & (x < l + float(MARGIN)))
    recip[...] = 1.0 / count

    lane = _iota((ROWS, LANES), 1)

    def pack_edges(s, c, plane):
        right = jnp.zeros((ROWS, LANES), F32)
        left_side = jnp.zeros((ROWS, LANES), F32)
        for z in range(NZ):
            here = lax.div(lane, EDGE) == z
            field = plane(z)
            right = jnp.where(
                here, pltpu.roll(field[:, COLS - LANES :], (EDGE * z + EDGE) % LANES, 1), right
            )
            left_side = jnp.where(here, pltpu.roll(field[:, :LANES], EDGE * z, 1), left_side)
        pack_right[s, c] = right.astype(BF16)
        pack_left[s, c] = left_side.astype(BF16)

    @pl.loop(0, CH)
    def _(c):
        for copy in [lower_copy(c), far_copy(c), *join_copies(c)]:
            copy.wait_recv()
        for z in range(NZ):
            total = own[c, z].astype(F32) + has_north * low_recv[c, z].astype(F32)
            spill = has_west * (
                side_recv[c, 0, z // 2].astype(F32) + has_north * side_recv[c, 1, z // 2].astype(F32)
            )
            if z % 2:
                spill = pltpu.roll(spill, 64, 1)
            spill = jnp.where(lane < 64, spill, 0.0)
            total = jnp.concatenate([total[:, :LANES] + spill, total[:, LANES:]], axis=1)
            value = total * recip[...]
            joined[c, z] = value
            est_ref[c, z] = value
            cur[0, c, z] = value.astype(BF16)
        pack_edges(0, c, lambda z: joined[c, z])
        start(edge_copies(0, c))
        start(row_copies(0, c))

    wide_lane = _iota((ROWS + 2 * EDGE, LANES), 1)
    from_west = (wide_lane >= LANES - EDGE) & (gx > 0)
    from_east = (wide_lane < EDGE) & (gx < n_gx - 1)

    def unpack_edges(s, c):
        west_side = left_recv[s, c].astype(F32)
        east_side = right_recv[s, c].astype(F32)
        for z in range(NZ):
            tile = jnp.where(
                from_west,
                pltpu.roll(west_side, (2 * LANES - EDGE - EDGE * z) % LANES, 1),
                jnp.where(from_east, pltpu.roll(east_side, (LANES - EDGE * z) % LANES, 1), 0.0),
            ).astype(BF16)
            edge[z * ROWS : (z + 1) * ROWS] = tile[:ROWS]
            edge[OWN + z * EDGE : OWN + (z + 1) * EDGE] = tile[ROWS : ROWS + EDGE]
            edge[OWN + STRIP + z * EDGE : OWN + STRIP + (z + 1) * EDGE] = tile[ROWS + EDGE :]

    def segments(s, c):
        return (
            (0, OWN, cur[s, c].reshape(OWN, COLS)),
            (OWN, 2 * STRIP, strip_recv[s, c].reshape(2 * STRIP, COLS)),
        )

    def blur(d, s, c):
        unpack_edges(s, c)
        taps = mat_x[d, c]
        for begin, size, field in segments(s, c):
            side = edge[begin : begin + size]
            first = jnp.concatenate([side, field[:, : COLS - LANES]], axis=1)
            spread[begin : begin + size, :half] = dot(first, taps).astype(BF16)
            second = jnp.concatenate([field[:, LANES:], side], axis=1)
            spread[begin : begin + size, half:] = dot(second, taps).astype(BF16)

    last = STEPS - 1

    def iterate(it, d, final):
        s = 2 * it + d
        rows = EDGE // 2 if final else EDGE

        @pl.loop(0, CH)
        def _(c):
            arrived(s, c)
            blur(d, s, c)
            seen = dot(mat_zy[d, c], spread[...]).reshape(NZ, ROWS, COLS)
            if d == 0:
                value = joined[c] / seen
            else:
                value = est_ref[c] * seen
                est_ref[c] = value
            cur[s + 1, c] = value.astype(BF16)
            pack_edges(s + 1, c, lambda z: cur[s + 1, c, z].astype(F32))
            for copy in edge_copies(s, c) + row_copies(s, c):
                copy.wait_send()
            start(edge_copies(s + 1, c, rows))
            start(row_copies(s + 1, c, rows))

    def join_sent():
        for copy in info_copies():
            copy.wait_send()

        @pl.loop(0, CH)
        def _(c):
            for copy in [lower_copy(c), *join_copies(c)]:
                copy.wait_send()

            @pl.when(odd)
            def _():
                for hop in range(3):
                    relay_copy(c, hop).wait_send()

            @pl.when(jnp.logical_not(odd))
            def _():
                far_copy(c).wait_send()

    for it in range(ITERS):
        iterate(it, 0, False)
        if it == 0:
            join_sent()
        iterate(it, 1, it == ITERS - 1)

    for copy in constant_loads:
        copy.wait()
    rows_of = jnp.where(gy == 0, prow_in[1], jnp.where(gy == n_gy - 1, prow_in[2], prow_in[0]))
    cols_of = jnp.where(gx == 0, ptwo_in[1], jnp.where(gx == n_gx - 1, ptwo_in[2], ptwo_in[0]))
    n_one = NZ * ROWS // 4

    @pl.loop(0, CH)
    def _(c):
        arrived(last, c, EDGE // 2)
        unpack_edges(last, c)
        main = jnp.zeros((rows_of.shape[0], COLS), F32)
        for begin, size, field in segments(last, c):
            main = main + dot(rows_of[:, begin : begin + size], field)
        side = dot(rows_of, edge[...])
        tall = jnp.concatenate([side, main], axis=1)
        high = tall.astype(BF16)
        low = (tall - high.astype(F32)).astype(BF16)
        one = dot(high[:n_one], pone_in[...]) + dot(low[:n_one], pone_in[...])
        one_ref[c] = one.reshape(NZ // 2, ROWS // 2, COLS // 2)
        two = dot(high[n_one:], cols_of) + dot(low[n_one:], cols_of)
        two_ref[c] = two.reshape(NZ // 4, ROWS // 4, COLS // 4)
        for copy in row_copies(last, c, EDGE // 2) + edge_copies(last, c, EDGE // 2):
            copy.wait_send()

def _settle(*refs):
    sem = refs[-1]
    pairs = [(refs[0].at[c, z], refs[3].at[c, z]) for c in range(CH) for z in (pl.ds(0, 4), pl.ds(4, 4))]
    pairs += [(refs[1], refs[4]), (refs[2], refs[5])]
    copies = [pltpu.make_async_copy(src, dst, sem.at[n]) for n, (src, dst) in enumerate(pairs)]
    for copy in copies:
        copy.start()
    for copy in copies:
        copy.wait()


def solution(mesh):

    sizes = (mesh.shape["gx"], mesh.shape["gy"])
    prow = _pyramid_rows()
    pone, ptwo = _pyramid_cols()
    vmem = pl.BlockSpec(memory_space=pltpu.VMEM)
    hbm = pl.BlockSpec(memory_space=pltpu.HBM)
    dma = pltpu.SemaphoreType.DMA

    def per_device(tiles, offsets, psf):
        outs = pl.pallas_call(
            functools.partial(_kernel, sizes),
            out_shape=(
                pltpu.VMEM((CH, NZ, ROWS, COLS), F32),
                pltpu.VMEM((CH, NZ // 2, ROWS // 2, COLS // 2), F32),
                pltpu.VMEM((CH, NZ // 4, ROWS // 4, COLS // 4), F32),
            ),
            in_specs=[hbm, hbm, hbm, hbm, hbm, hbm],
            out_specs=(vmem, vmem, vmem),
            scratch_shapes=[
                pltpu.SMEM((1, 1, 2), jnp.int32),
                pltpu.SMEM((CH, 3, TAPS), F32),
                pltpu.VMEM((CH, NZ, TROWS, TCOLS), BF16),
                pltpu.VMEM(prow.shape, BF16),
                pltpu.VMEM(pone.shape, BF16),
                pltpu.VMEM(ptwo.shape, BF16),
                pltpu.VMEM((NZ * TROWS, COLS + LANES), BF16),
                pltpu.VMEM((CH, NZ, ROWS, COLS), BF16),
                pltpu.VMEM((CH, NZ, ROWS, COLS), BF16),
                pltpu.VMEM((CH, NZ, ROWS, COLS), BF16),
                pltpu.VMEM((CH, 2, NZ // 2, ROWS, LANES), BF16),
                pltpu.VMEM((CH, 2, NZ // 2, ROWS, LANES), BF16),
                pltpu.VMEM((16, LANES), F32),
                pltpu.VMEM((3, 16, LANES), F32),
                pltpu.VMEM((ROWS, COLS), F32),
                pltpu.VMEM((CH, NZ, ROWS, COLS), F32),
                pltpu.VMEM((STEPS, CH, NZ, ROWS, COLS), BF16),
                pltpu.VMEM((STEPS, CH, 2, NZ, EDGE, COLS), BF16),
                pltpu.VMEM((STEPS, CH, ROWS, LANES), BF16),
                pltpu.VMEM((STEPS, CH, ROWS, LANES), BF16),
                pltpu.VMEM((STEPS, CH, ROWS + 2 * EDGE, LANES), BF16),
                pltpu.VMEM((STEPS, CH, ROWS + 2 * EDGE, LANES), BF16),
                pltpu.VMEM((ALL, LANES), BF16),
                pltpu.VMEM((ALL, COLS), BF16),
                pltpu.VMEM((2, CH, COLS, COLS // 2), BF16),
                pltpu.VMEM((2, CH, OWN, ALL), BF16),
                dma((CH + 5,)),
                dma((CH, 3)),
                dma((CH, 3)),
                pltpu.VMEM((CH, 2, RELAY, ROWS, COLS), BF16),
                dma((CH, 3)),
                dma((CH, 3)),
                dma((3,)),
                dma((3,)),
                dma((CH, 8)),
                dma((2, CH, 3)),
            ],
            compiler_params=pltpu.CompilerParams(
                collective_id=0, has_side_effects=True, vmem_limit_bytes=48 * 1024 * 1024
            ),
        )(*[
            pltpu.with_memory_space_constraint(x, pltpu.HBM)
            for x in (offsets, psf, tiles, jnp.asarray(prow), jnp.asarray(pone), jnp.asarray(ptwo))
        ])
        return pl.pallas_call(
            _settle,
            out_shape=tuple(jax.ShapeDtypeStruct(o.shape, o.dtype) for o in outs),
            in_specs=[vmem] * 3,
            out_specs=(hbm,) * 3,
            scratch_shapes=[dma((2 * CH + 2,))],
            compiler_params=pltpu.CompilerParams(vmem_limit_bytes=4 * 1024 * 1024),
        )(*[pltpu.with_memory_space_constraint(o, pltpu.VMEM) for o in outs])

    in_specs = (P(None, None, "gy", "gx"), P("gy", "gx", None), P())
    out_specs = (P(None, None, "gy", "gx"),) * 3
    return jax.shard_map(
        per_device, mesh=mesh, in_specs=in_specs, out_specs=out_specs, check_vma=False
    )
```

```python
import functools

import jax
import jax.numpy as jnp
import numpy as np
from jax import lax
from jax.experimental import pallas as pl
from jax.experimental.pallas import tpu as pltpu
from jax.sharding import PartitionSpec as P

MESH = pl.DeviceIdType.MESH
F32 = jnp.float32
BF16 = jnp.bfloat16

CH, NZ, ROWS, COLS = 3, 8, 64, 512
MARGIN = 32
TROWS, TCOLS = ROWS + MARGIN, COLS + MARGIN
TAPS, HALF = 31, 15
ITERS = 2
STEPS = 2 * ITERS + 1
EDGE = 16
RELAY = 2
LANES = 128
OWN, STRIP = NZ * ROWS, NZ * EDGE
ALL = OWN + 2 * STRIP

GAUSS = np.array([1.0, 4.0, 6.0, 4.0, 1.0]) / 16.0


def _shrink(size_out, inputs):
    tap = np.asarray(inputs)[None, :] - 2 * np.arange(size_out)[:, None] + 2
    return np.where((tap >= 0) & (tap < 5), GAUSS[np.clip(tap, 0, 4)], 0.0)


def _shrink_twice(size_out, inputs, low_edge, high_edge):
    mid = np.arange(-2, 2 * size_out + 1)
    first = np.asarray(inputs)[None, :] - 2 * mid[:, None] + 2
    first = np.where((first >= 0) & (first < 5), GAUSS[np.clip(first, 0, 4)], 0.0)
    second = mid[None, :] - 2 * np.arange(size_out)[:, None] + 2
    second = np.where((second >= 0) & (second < 5), GAUSS[np.clip(second, 0, 4)], 0.0)
    keep = np.ones(mid.size)
    if low_edge:
        keep[mid < 0] = 0.0
    if high_edge:
        keep[mid >= 2 * size_out] = 0.0
    return second @ (keep[:, None] * first)


def _pyramid_rows():
    z_in = np.arange(NZ)
    z_one = _shrink(NZ // 2, z_in)
    z_two = _shrink(NZ // 4, np.arange(NZ // 2)) @ z_one
    parts = []
    for low, high in ((False, False), (True, False), (False, True)):
        blocks = []
        for coords, live in (
            (np.arange(ROWS), True),
            (np.arange(-EDGE, 0), not low),
            (np.arange(ROWS, ROWS + EDGE), not high),
        ):
            one = _shrink(ROWS // 2, coords) * live
            two = _shrink_twice(ROWS // 4, coords, low, high) * live
            blocks.append(np.concatenate([np.kron(z_one, one), np.kron(z_two, two)], axis=0))
        parts.append(np.concatenate(blocks, axis=1))
    return np.stack(parts).astype(jnp.bfloat16)


def _pyramid_cols():
    lane = np.arange(LANES)
    far = 10 * COLS
    edge = np.where(lane >= LANES - EDGE, lane - LANES, np.where(lane < EDGE, COLS + lane, far))
    coords = np.concatenate([edge, np.arange(COLS)])
    one = _shrink(COLS // 2, coords).T
    twos = [
        _shrink_twice(COLS // 4, coords, low, high).T
        for low, high in ((False, False), (True, False), (False, True))
    ]
    return one.astype(jnp.bfloat16), np.stack(twos).astype(jnp.bfloat16)


def _iota(shape, dim):
    return lax.broadcasted_iota(jnp.int32, shape, dim)


def _kernel(
    sizes,
    offsets_in,
    psf_in,
    tiles_ref,
    prow_ref,
    pone_ref,
    ptwo_ref,
    est_ref,
    one_ref,
    two_ref,
    offsets_ref,
    psf_ref,
    tiles_in,
    prow_in,
    pone_in,
    ptwo_in,
    shifted,
    own,
    low_send,
    low_recv,
    side_send,
    side_recv,
    info_send,
    info_recv,
    recip,
    joined,
    cur,
    strip_recv,
    pack_right,
    pack_left,
    left_recv,
    right_recv,
    edge,
    spread,
    mat_x,
    mat_zy,
    load_sem,
    join_recv_sem,
    relay,
    relay_recv_sem,
    info_send_sem,
    info_recv_sem,
    send_sem,
    recv_sem,
):
    n_gx, n_gy = sizes
    gx, gy = lax.axis_index("gx"), lax.axis_index("gy")
    east, west = lax.rem(gx + 1, n_gx), lax.rem(gx + n_gx - 1, n_gx)
    south, north = lax.rem(gy + 1, n_gy), lax.rem(gy + n_gy - 1, n_gy)

    def at(x, y):
        return {"gx": x, "gy": y}

    around = [
        at(east, gy),
        at(west, gy),
        at(gx, south),
        at(gx, north),
        at(east, south),
        at(east, north),
        at(west, south),
        at(west, north),
    ]
    odd = lax.rem(gy, 2) == 1
    ring = [at(gx, lax.rem(gy + k, n_gy)) for k in (n_gy - 2, n_gy - 3, 2, 3)]
    barrier = pltpu.get_barrier_semaphore()
    for place in around + ring:
        pl.semaphore_signal(barrier, inc=1, device_id=place, device_id_type=MESH)

    tile_loads = [
        pltpu.make_async_copy(tiles_ref.at[c], tiles_in.at[c], load_sem.at[c]) for c in range(CH)
    ]
    constant_loads = [
        pltpu.make_async_copy(src, dst, load_sem.at[CH + n])
        for n, (src, dst) in enumerate(
            ((prow_ref, prow_in), (pone_ref, pone_in), (ptwo_ref, ptwo_in))
        )
    ]
    offsets_load = pltpu.make_async_copy(offsets_in, offsets_ref, load_sem.at[CH + 3])
    psf_load = pltpu.make_async_copy(psf_in, psf_ref, load_sem.at[CH + 4])
    for copy in [offsets_load, *tile_loads, psf_load, *constant_loads]:
        copy.start()

    def remote(src, dst, send, recv, place):
        return pltpu.make_async_remote_copy(
            src_ref=src, dst_ref=dst, send_sem=send, recv_sem=recv, device_id=place, device_id_type=MESH
        )

    def join_copies(c):
        return [
            remote(side_send.at[c, 0], side_recv.at[c, 0], send_sem.at[c, 1], join_recv_sem.at[c, 1], around[0]),
            remote(side_send.at[c, 1], side_recv.at[c, 1], send_sem.at[c, 2], join_recv_sem.at[c, 2], around[4]),
        ]

    def lower_copy(c, planes=slice(0, NZ - RELAY)):
        z = pl.ds(planes.start, planes.stop - planes.start)
        return remote(
            low_send.at[c, z], low_recv.at[c, z], send_sem.at[c, 0], join_recv_sem.at[c, 0], around[2]
        )

    far = pl.ds(NZ - RELAY, RELAY)

    def far_copy(c):
        return remote(
            low_send.at[c, far], low_recv.at[c, far], send_sem.at[c, 3], relay_recv_sem.at[c, 0], around[2]
        )

    def relay_copy(c, hop):
        src = low_send.at[c, far] if hop == 0 else relay.at[c, hop - 1]
        dst = low_recv.at[c, far] if hop == 2 else relay.at[c, hop]
        return remote(
            src,
            dst,
            send_sem.at[c, 3 + hop],
            relay_recv_sem.at[c, 0 if hop == 2 else hop + 1],
            ring[1] if hop == 2 else ring[0],
        )

    def info_copies():
        return [
            remote(info_send, info_recv.at[n], info_send_sem.at[n], info_recv_sem.at[n], around[k])
            for n, k in enumerate((0, 2, 4))
        ]

    def row_copies(s, c, rows=EDGE):
        parts = [
            (pl.ds(ROWS - rows, rows), 0, pl.ds(EDGE - rows, rows), around[2]),
            (pl.ds(0, rows), 1, pl.ds(0, rows), around[3]),
        ]
        return [
            remote(
                cur.at[s, c, :, src],
                strip_recv.at[s, c, n, :, dst],
                send_sem.at[c, n],
                recv_sem.at[s % 2, c, n],
                place,
            )
            for src, n, dst, place in parts
        ]

    def edge_copies(s, c, rows=EDGE):
        first, last, main = pl.ds(0, rows), pl.ds(ROWS - rows, rows), pl.ds(0, ROWS)
        upper, lower = pl.ds(ROWS + EDGE - rows, rows), pl.ds(ROWS + EDGE, rows)
        right, left = pack_right.at[s, c], pack_left.at[s, c]
        parts = [
            (pack_right.at[s, c, last], left_recv.at[s, c, upper], around[4]),
            (pack_right.at[s, c, first], left_recv.at[s, c, lower], around[5]),
            (pack_left.at[s, c, last], right_recv.at[s, c, upper], around[6]),
            (pack_left.at[s, c, first], right_recv.at[s, c, lower], around[7]),
            (right, left_recv.at[s, c, main], around[0]),
            (left, right_recv.at[s, c, main], around[1]),
        ]
        return [
            remote(src, dst, send_sem.at[c, 2 + n], recv_sem.at[s % 2, c, 2 + n], place)
            for n, (src, dst, place) in enumerate(parts)
        ]

    def start(copies):
        for copy in copies:
            copy.start()

    offsets_load.wait()
    top = offsets_ref[0, 0, 0]
    left = offsets_ref[0, 0, 1]
    info_send[0:8] = jnp.full((8, LANES), top.astype(F32), F32)
    info_send[8:16] = jnp.full((8, LANES), left.astype(F32), F32)

    def one_hot(cond):
        return jnp.where(cond, 1.0, 0.0).astype(BF16)

    half = COLS // 2
    shift_a = one_hot(_iota((half, half), 1) - _iota((half, half), 0) == left)
    shift_b = one_hot(_iota((384, half), 1) - _iota((384, half), 0) + LANES == left)
    shift_c = one_hot(_iota((160, LANES), 1) - _iota((160, LANES), 0) + LANES == left)
    row, col = _iota((4 * ROWS, 2 * TROWS), 0), _iota((4 * ROWS, 2 * TROWS), 1)
    row_odd = lax.rem(row, 2 * ROWS) >= ROWS
    col_odd = col >= TROWS
    row_at = lax.rem(row, ROWS) + jnp.where(row >= 2 * ROWS, ROWS, 0)
    col_at = col - jnp.where(col_odd, TROWS, 0)
    lower_it = one_hot((row_odd == col_odd) & (row_at - col_at == top))

    def dot(a, b):
        return jnp.dot(a, b, preferred_element_type=F32)

    unused = jnp.zeros((CH, NZ, EDGE // 2, COLS), BF16)
    strip_recv[STEPS - 1, :, 0, :, : EDGE // 2] = unused
    strip_recv[STEPS - 1, :, 1, :, EDGE // 2 :] = unused
    unused = jnp.zeros((CH, EDGE // 2, LANES), BF16)
    for side_recv_ref in (left_recv, right_recv):
        side_recv_ref[STEPS - 1, :, ROWS : ROWS + EDGE // 2] = unused
        side_recv_ref[STEPS - 1, :, ROWS + EDGE + EDGE // 2 :] = unused


    pairs = (NZ // 2 - 1, *range(NZ // 2 - 1))

    def place_tile(c, then):
        pltpu.make_async_copy(tiles_ref.at[c], tiles_in.at[c], load_sem.at[c]).wait()
        tile = tiles_in[c].reshape(NZ * TROWS, TCOLS)
        shifted[:, 0:half] = dot(tile[:, 0:half], shift_a).astype(BF16)
        shifted[:, half:COLS] = dot(tile[:, LANES:COLS], shift_b).astype(BF16)
        shifted[:, COLS:] = dot(tile[:, COLS - LANES :], shift_c).astype(BF16)
        for p in pairs:
            placed = dot(lower_it, shifted[2 * p * TROWS : 2 * (p + 1) * TROWS, :])
            for zz in range(2):
                own[c, 2 * p + zz] = placed[zz * ROWS : (zz + 1) * ROWS, :COLS].astype(BF16)
                low_send[c, 2 * p + zz] = placed[(2 + zz) * ROWS : (3 + zz) * ROWS, :COLS].astype(BF16)
            for part in range(2):
                even = placed[2 * part * ROWS : (2 * part + 1) * ROWS, COLS:]
                second = placed[(2 * part + 1) * ROWS : (2 * part + 2) * ROWS, COLS:]
                side_send[c, part, p] = (even + pltpu.roll(second, 64, 1)).astype(BF16)
            then(p)

    def send_rows(c, p):
        if 2 * p < NZ - RELAY:
            lower_copy(c, slice(2 * p, 2 * p + 2)).start()
        else:

            @pl.when(odd)
            def _():
                relay_copy(c, 0).start()

            @pl.when(jnp.logical_not(odd))
            def _():
                far_copy(c).start()

    place_tile(0, lambda p: None)
    pl.semaphore_wait(barrier, len(around) + len(ring))
    start(info_copies())
    for p in pairs:
        send_rows(0, p)
    start(join_copies(0))

    @pl.loop(1, CH)
    def _(c):
        place_tile(c, lambda p: send_rows(c, p))
        start(join_copies(c))

    psf_load.wait()

    @pl.loop(0, CH)
    def _(c):
        def total(a):
            t = psf_ref[c, a, 0]
            for k in range(1, TAPS):
                t = t + psf_ref[c, a, k]
            return t

        inv_x = 1.0 / jnp.full((1, LANES), total(2), F32)
        inv_zy = 1.0 / jnp.full((1, LANES), total(0) * total(1), F32)

        def banded(axis, diff, ks=range(TAPS)):
            ahead = jnp.zeros(diff.shape, F32)
            back = jnp.zeros(diff.shape, F32)
            for k in ks:
                hit = diff == k
                ahead = jnp.where(hit, psf_ref[c, axis, k], ahead)
                back = jnp.where(hit, psf_ref[c, axis, TAPS - 1 - k], back)
            return ahead, back

        square = (LANES, LANES)
        across = _iota(square, 0) - _iota(square, 1)
        for a, shift in enumerate((-113, 15, 143)):
            for d, block in enumerate(banded(2, across + shift)):
                block = (block * inv_x).astype(BF16)
                mat_x[d, c, a * LANES : (a + 1) * LANES, 0:LANES] = block
                mat_x[d, c, (a + 1) * LANES : (a + 2) * LANES, LANES:] = block
        zero = jnp.zeros(square, BF16)
        for d in range(2):
            mat_x[d, c, 0:LANES, LANES:] = zero
            mat_x[d, c, 3 * LANES :, 0:LANES] = zero

        yo = _iota((ROWS, LANES), 0)
        lane = _iota((ROWS, LANES), 1)
        inner = banded(1, lax.rem(lane, ROWS) - yo + HALF)
        above = banded(1, lax.rem(lane, EDGE) - EDGE - yo + HALF)
        below = banded(1, lax.rem(lane, EDGE) + ROWS - yo + HALF)
        has_above = jnp.where(gy > 0, 1.0, 0.0).astype(F32)
        has_below = jnp.where(gy < n_gy - 1, 1.0, 0.0).astype(F32)
        zo = _iota((NZ, LANES), 0)
        zlane = _iota((NZ, LANES), 1)
        depth_taps = range(HALF - NZ + 1, HALF + NZ)
        depth_own = [
            banded(0, 2 * j + lax.div(zlane, ROWS) - zo + HALF, depth_taps) for j in range(4)
        ]
        depth_edge = banded(0, lax.div(zlane, EDGE) - zo + HALF, depth_taps)
        for d in range(2):
            y_own = inner[d] * inv_zy
            y_above = above[d] * inv_zy * has_above
            y_below = below[d] * inv_zy * has_below
            for z in range(NZ):
                at_rows = slice(z * ROWS, (z + 1) * ROWS)
                for j in range(4):
                    mat_zy[d, c, at_rows, j * LANES : (j + 1) * LANES] = (
                        y_own * depth_own[j][d][z : z + 1]
                    ).astype(BF16)
                mat_zy[d, c, at_rows, 4 * LANES : 5 * LANES] = (
                    y_above * depth_edge[d][z : z + 1]
                ).astype(BF16)
                mat_zy[d, c, at_rows, 5 * LANES :] = (y_below * depth_edge[d][z : z + 1]).astype(BF16)

        @pl.when(odd)
        def _():
            relay_copy(c, 0).wait_recv()
            relay_copy(c, 1).start()

    @pl.when(odd)
    def _():
        @pl.loop(0, CH)
        def _(c):
            relay_copy(c, 1).wait_recv()
            relay_copy(c, 2).start()

    for copy in info_copies():
        copy.wait_recv()
    has_west = jnp.where(gx > 0, 1.0, 0.0).astype(F32)
    has_north = jnp.where(gy > 0, 1.0, 0.0).astype(F32)
    r = _iota((ROWS, COLS), 0).astype(F32)
    x = _iota((ROWS, COLS), 1).astype(F32)

    def told(n):
        t = jnp.broadcast_to(info_recv[n, 0:1, 0:1], (ROWS, COLS))
        l = jnp.broadcast_to(info_recv[n, 8:9, 0:1], (ROWS, COLS))
        return t, l

    def covers(cond):
        return jnp.where(cond, 1.0, 0.0)

    count = covers((r >= top.astype(F32)) & (x >= left.astype(F32)))
    t, l = told(0)
    count = count + has_west * covers((r >= t) & (x < l + float(MARGIN)))
    t, l = told(1)
    count = count + has_north * covers((r < t + float(MARGIN)) & (x >= l))
    t, l = told(2)
    count = count + has_west * has_north * covers((r < t + float(MARGIN)) & (x < l + float(MARGIN)))
    recip[...] = 1.0 / count

    lane = _iota((ROWS, LANES), 1)

    def pack_edges(s, c, plane):
        right = jnp.zeros((ROWS, LANES), F32)
        left_side = jnp.zeros((ROWS, LANES), F32)
        for z in range(NZ):
            here = lax.div(lane, EDGE) == z
            field = plane(z)
            right = jnp.where(
                here, pltpu.roll(field[:, COLS - LANES :], (EDGE * z + EDGE) % LANES, 1), right
            )
            left_side = jnp.where(here, pltpu.roll(field[:, :LANES], EDGE * z, 1), left_side)
        pack_right[s, c] = right.astype(BF16)
        pack_left[s, c] = left_side.astype(BF16)

    @pl.loop(0, CH)
    def _(c):
        for copy in [lower_copy(c), far_copy(c), *join_copies(c)]:
            copy.wait_recv()
        for z in range(NZ):
            total = own[c, z].astype(F32) + has_north * low_recv[c, z].astype(F32)
            spill = has_west * (
                side_recv[c, 0, z // 2].astype(F32) + has_north * side_recv[c, 1, z // 2].astype(F32)
            )
            if z % 2:
                spill = pltpu.roll(spill, 64, 1)
            spill = jnp.where(lane < 64, spill, 0.0)
            total = jnp.concatenate([total[:, :LANES] + spill, total[:, LANES:]], axis=1)
            value = total * recip[...]
            joined[c, z] = value
            est_ref[c, z] = value
            cur[0, c, z] = value.astype(BF16)
        pack_edges(0, c, lambda z: joined[c, z])
        for copy in [lower_copy(c), *join_copies(c)]:
            copy.wait_send()

        @pl.when(odd)
        def _():
            for hop in range(3):
                relay_copy(c, hop).wait_send()

        @pl.when(jnp.logical_not(odd))
        def _():
            far_copy(c).wait_send()

        start(edge_copies(0, c))
        start(row_copies(0, c))

    wide_lane = _iota((ROWS + 2 * EDGE, LANES), 1)
    from_west = (wide_lane >= LANES - EDGE) & (gx > 0)
    from_east = (wide_lane < EDGE) & (gx < n_gx - 1)

    def unpack_edges(s, c):
        west_side = left_recv[s, c].astype(F32)
        east_side = right_recv[s, c].astype(F32)
        for z in range(NZ):
            tile = jnp.where(
                from_west,
                pltpu.roll(west_side, (2 * LANES - EDGE - EDGE * z) % LANES, 1),
                jnp.where(from_east, pltpu.roll(east_side, (LANES - EDGE * z) % LANES, 1), 0.0),
            ).astype(BF16)
            edge[z * ROWS : (z + 1) * ROWS] = tile[:ROWS]
            edge[OWN + z * EDGE : OWN + (z + 1) * EDGE] = tile[ROWS : ROWS + EDGE]
            edge[OWN + STRIP + z * EDGE : OWN + STRIP + (z + 1) * EDGE] = tile[ROWS + EDGE :]

    def segments(s, c):
        return (
            (0, OWN, cur[s, c].reshape(OWN, COLS)),
            (OWN, 2 * STRIP, strip_recv[s, c].reshape(2 * STRIP, COLS)),
        )

    def blur(d, s, c):
        unpack_edges(s, c)
        taps = mat_x[d, c]
        for begin, size, field in segments(s, c):
            side = edge[begin : begin + size]
            first = jnp.concatenate([side, field[:, : COLS - LANES]], axis=1)
            spread[begin : begin + size, :half] = dot(first, taps).astype(BF16)
            second = jnp.concatenate([field[:, LANES:], side], axis=1)
            spread[begin : begin + size, half:] = dot(second, taps).astype(BF16)

    last = STEPS - 1

    def iterate(it, d, final):
        s = 2 * it + d
        rows = EDGE // 2 if final else EDGE

        @pl.loop(0, CH)
        def _(c):
            for copy in row_copies(s, c) + edge_copies(s, c):
                copy.wait_recv()
            blur(d, s, c)
            seen = dot(mat_zy[d, c], spread[...]).reshape(NZ, ROWS, COLS)
            if d == 0:
                value = joined[c] / seen
            else:
                value = est_ref[c] * seen
                est_ref[c] = value
            cur[s + 1, c] = value.astype(BF16)
            pack_edges(s + 1, c, lambda z: cur[s + 1, c, z].astype(F32))
            for copy in edge_copies(s, c) + row_copies(s, c):
                copy.wait_send()
            start(edge_copies(s + 1, c, rows))
            start(row_copies(s + 1, c, rows))

    for it in range(ITERS):
        iterate(it, 0, False)
        iterate(it, 1, it == ITERS - 1)

    for copy in info_copies():
        copy.wait_send()

    for copy in constant_loads:
        copy.wait()
    rows_of = jnp.where(gy == 0, prow_in[1], jnp.where(gy == n_gy - 1, prow_in[2], prow_in[0]))
    cols_of = jnp.where(gx == 0, ptwo_in[1], jnp.where(gx == n_gx - 1, ptwo_in[2], ptwo_in[0]))
    n_one = NZ * ROWS // 4

    @pl.loop(0, CH)
    def _(c):
        for copy in row_copies(last, c, EDGE // 2) + edge_copies(last, c, EDGE // 2):
            copy.wait_recv()
        unpack_edges(last, c)
        main = jnp.zeros((rows_of.shape[0], COLS), F32)
        for begin, size, field in segments(last, c):
            main = main + dot(rows_of[:, begin : begin + size], field)
        side = dot(rows_of, edge[...])
        tall = jnp.concatenate([side, main], axis=1)
        high = tall.astype(BF16)
        low = (tall - high.astype(F32)).astype(BF16)
        one = dot(high[:n_one], pone_in[...]) + dot(low[:n_one], pone_in[...])
        one_ref[c] = one.reshape(NZ // 2, ROWS // 2, COLS // 2)
        two = dot(high[n_one:], cols_of) + dot(low[n_one:], cols_of)
        two_ref[c] = two.reshape(NZ // 4, ROWS // 4, COLS // 4)
        for copy in row_copies(last, c, EDGE // 2) + edge_copies(last, c, EDGE // 2):
            copy.wait_send()

def _settle(*refs):
    sem = refs[-1]
    pairs = [(refs[n], refs[n + 3]) for n in range(3)]
    copies = [pltpu.make_async_copy(src, dst, sem.at[n]) for n, (src, dst) in enumerate(pairs)]
    for copy in copies:
        copy.start()
    for copy in copies:
        copy.wait()


def solution(mesh):

    sizes = (mesh.shape["gx"], mesh.shape["gy"])
    prow = _pyramid_rows()
    pone, ptwo = _pyramid_cols()
    vmem = pl.BlockSpec(memory_space=pltpu.VMEM)
    hbm = pl.BlockSpec(memory_space=pltpu.HBM)
    dma = pltpu.SemaphoreType.DMA

    def per_device(tiles, offsets, psf):
        outs = pl.pallas_call(
            functools.partial(_kernel, sizes),
            out_shape=(
                pltpu.VMEM((CH, NZ, ROWS, COLS), F32),
                pltpu.VMEM((CH, NZ // 2, ROWS // 2, COLS // 2), F32),
                pltpu.VMEM((CH, NZ // 4, ROWS // 4, COLS // 4), F32),
            ),
            in_specs=[hbm, hbm, hbm, hbm, hbm, hbm],
            out_specs=(vmem, vmem, vmem),
            scratch_shapes=[
                pltpu.SMEM((1, 1, 2), jnp.int32),
                pltpu.SMEM((CH, 3, TAPS), F32),
                pltpu.VMEM((CH, NZ, TROWS, TCOLS), BF16),
                pltpu.VMEM(prow.shape, BF16),
                pltpu.VMEM(pone.shape, BF16),
                pltpu.VMEM(ptwo.shape, BF16),
                pltpu.VMEM((NZ * TROWS, COLS + LANES), BF16),
                pltpu.VMEM((CH, NZ, ROWS, COLS), BF16),
                pltpu.VMEM((CH, NZ, ROWS, COLS), BF16),
                pltpu.VMEM((CH, NZ, ROWS, COLS), BF16),
                pltpu.VMEM((CH, 2, NZ // 2, ROWS, LANES), BF16),
                pltpu.VMEM((CH, 2, NZ // 2, ROWS, LANES), BF16),
                pltpu.VMEM((16, LANES), F32),
                pltpu.VMEM((3, 16, LANES), F32),
                pltpu.VMEM((ROWS, COLS), F32),
                pltpu.VMEM((CH, NZ, ROWS, COLS), F32),
                pltpu.VMEM((STEPS, CH, NZ, ROWS, COLS), BF16),
                pltpu.VMEM((STEPS, CH, 2, NZ, EDGE, COLS), BF16),
                pltpu.VMEM((STEPS, CH, ROWS, LANES), BF16),
                pltpu.VMEM((STEPS, CH, ROWS, LANES), BF16),
                pltpu.VMEM((STEPS, CH, ROWS + 2 * EDGE, LANES), BF16),
                pltpu.VMEM((STEPS, CH, ROWS + 2 * EDGE, LANES), BF16),
                pltpu.VMEM((ALL, LANES), BF16),
                pltpu.VMEM((ALL, COLS), BF16),
                pltpu.VMEM((2, CH, COLS, COLS // 2), BF16),
                pltpu.VMEM((2, CH, OWN, ALL), BF16),
                dma((CH + 5,)),
                dma((CH, 3)),
                pltpu.VMEM((CH, 2, RELAY, ROWS, COLS), BF16),
                dma((CH, 3)),
                dma((3,)),
                dma((3,)),
                dma((CH, 8)),
                dma((2, CH, 8)),
            ],
            compiler_params=pltpu.CompilerParams(
                collective_id=0, has_side_effects=True, vmem_limit_bytes=48 * 1024 * 1024
            ),
        )(*[
            pltpu.with_memory_space_constraint(x, pltpu.HBM)
            for x in (offsets, psf, tiles, jnp.asarray(prow), jnp.asarray(pone), jnp.asarray(ptwo))
        ])
        return pl.pallas_call(
            _settle,
            out_shape=tuple(jax.ShapeDtypeStruct(o.shape, o.dtype) for o in outs),
            in_specs=[vmem] * 3,
            out_specs=(hbm,) * 3,
            scratch_shapes=[dma((3,))],
            compiler_params=pltpu.CompilerParams(vmem_limit_bytes=4 * 1024 * 1024),
        )(*[pltpu.with_memory_space_constraint(o, pltpu.VMEM) for o in outs])

    in_specs = (P(None, None, "gy", "gx"), P("gy", "gx", None), P())
    out_specs = (P(None, None, "gy", "gx"),) * 3
    return jax.shard_map(
        per_device, mesh=mesh, in_specs=in_specs, out_specs=out_specs, check_vma=False
    )
```
